128 devices in a mesh: dp: 8 (over x, core), rows: 16 (over z, y).
Axes of the slice: x: 4, y: 4, z: 4, core: 2. Of those that a mesh axis runs over, the one named last changes fastest.
Arguments:
- item_table: float32 [524288, 128], P(('dp', 'rows')), may hold values from -3 to 3
- adagrad_state: float32 [524288, 128], P(('dp', 'rows')), may hold values from 0.0001 to 0.01
- history_ids: int32 [16384, 50], P(('dp', 'rows')), may hold values from 0 to 524287, as said below
- positive_ids: int32 [16384], P(('dp', 'rows')), may hold values from 0 to 524287, as said below
Outputs:
- new_table: float32 [524288, 128], P(('dp', 'rows'))
- new_state: float32 [524288, 128], P(('dp', 'rows'))
The draws below stay inside these ranges and needn't reach their ends.
Inputs may be any that keep to these rules, and one draw needn't show every extreme that they name: `history_ids`: ids are counted over one device's 128 users (an aligned block of users), history and positive together, with repeats. In every such block, at most 128 ids have any one value of id // 4096, and some value has exactly 128; one value has exactly 128 in every block. Popular items repeat. `positive_ids`: counted together with history_ids as stated there.
All inputs are finite; a program needn't handle non-finite values.
Results may differ from the reference program's by a relative error of at most 0.00012.
Values sent between devices are 32-bit elements; how exact they have to be, the bound alone decides.
No kernel may reach another device: no remote copies, remote signals or barrier semaphores. Data moves between devices by JAX's collectives and lax.ppermute only.
A program may use at most 128 MiB of HBM per device.

```python
import math
import jax
import jax.numpy as jnp
from jax import lax

EMB = 128
HIST = 50
USER_DEV = 128
ROW_DEV = 4096
USERS = 16384
ITEMS = 524288
CAP = 128


def request_ids(key):
    base = jax.random.fold_in(key, 7001)
    keys = jax.random.split(base, 7)
    blocks = USERS // USER_DEV
    slots = blocks * CAP
    per_block = USER_DEV * (HIST + 1)
    slot_owner = jnp.arange(slots, dtype=jnp.int32) // CAP
    noise = jax.random.randint(keys[0], (blocks, slots), 0, 1024, dtype=jnp.int32)
    level = jax.random.randint(keys[1], (blocks, blocks), 0, 4, dtype=jnp.int32) * 512
    hot_common = jax.random.randint(keys[2], (), 0, blocks, dtype=jnp.int32)
    hot_own = jax.random.randint(keys[3], (blocks,), 0, blocks, dtype=jnp.int32)
    hot_flag = jnp.logical_or(slot_owner[None, :] == hot_common, slot_owner[None, :] == hot_own[:, None]).astype(jnp.int32)
    score = (noise + level[:, slot_owner] + 8192 * hot_flag) * slots + jnp.arange(slots, dtype=jnp.int32)[None, :]
    picked_score, chosen = lax.top_k(score, per_block)
    owners = (chosen // CAP).astype(jnp.int32)
    order_keys = jax.random.randint(keys[4], (blocks, per_block), 0, 32768, dtype=jnp.int32) * per_block + jnp.arange(per_block, dtype=jnp.int32)[None, :]
    order = jnp.argsort(order_keys, axis=1, stable=True)
    owners = jnp.take_along_axis(owners, order, axis=1)
    first = jax.random.randint(keys[5], (blocks, per_block), 0, ROW_DEV, dtype=jnp.int32)
    second = jax.random.randint(keys[6], (blocks, per_block), 0, ROW_DEV, dtype=jnp.int32)
    offset = first * second // ROW_DEV
    return (owners * ROW_DEV + offset).astype(jnp.int32).reshape(USERS, HIST + 1)


def draw_history_ids(key, part):
    return request_ids(key)[:, :HIST]


def draw_positive_ids(key, part):
    return request_ids(key)[:, HIST]


def levels(stream_key, dims, cuts, least, high):
    def one(position, parts):
        heights = jax.random.uniform(jax.random.fold_in(jax.random.fold_in(stream_key, 6), position), (parts,), jnp.float32, least / len(cuts), high / len(cuts))
        return jnp.repeat(jnp.exp(heights), dims[position] // parts).reshape((-1,) + (1,) * (len(dims) - position - 1))

    gain = one(*cuts[0])
    for cut in cuts[1:]:
        gain = gain * one(*cut)
    return gain


def normal_values(own_key, dims, width, limit, cuts=(), kind=jnp.bfloat16):
    array = jax.random.normal(own_key, dims, jnp.float32) * width
    if len(cuts) > 0:
        array = levels(own_key, dims, cuts, -0.22, 0.18) * array
    return jnp.clip(array, min=-limit, max=limit).astype(kind)


def setup_inputs(seed: int = 0) -> dict:
    streams_of = jax.random.split(jax.random.key(seed), 5)
    return {
        "item_table": normal_values(streams_of[0], (ITEMS, EMB), 0.5, 3.0, ((0, 128),), jnp.float32),
        "adagrad_state": jnp.clip(jnp.exp(math.log(0.01) - 4.6051702 * jax.random.uniform(streams_of[1], (ITEMS, EMB), jnp.float32) ** levels(streams_of[1], (ITEMS, EMB), ((0, 128),), -0.2, 0.2)), 0.0001, 0.01),
        "history_ids": draw_history_ids(jax.random.fold_in(streams_of[4], 71), 0),
        "positive_ids": draw_positive_ids(jax.random.fold_in(streams_of[4], 71), 0),
    }


penalty_weight = 10.0
step_size = 0.05

def reference(item_table, adagrad_state, history_ids, positive_ids):
    hist_rows = jnp.take(item_table, history_ids, axis=0)
    user_vecs = lax.optimization_barrier(jnp.sum(hist_rows, axis=1)) / HIST
    positive_vecs = jnp.take(item_table, positive_ids, axis=0)
    score_gap = lax.optimization_barrier(jnp.sum(user_vecs * positive_vecs, axis=1)) - 1.0
    user_gram = jnp.dot(user_vecs.T, user_vecs, precision=lax.Precision.HIGHEST, preferred_element_type=jnp.float32)
    item_gram = jnp.dot(item_table.T, item_table, precision=lax.Precision.HIGHEST, preferred_element_type=jnp.float32)
    penalty_coef = penalty_weight / ITEMS
    user_grad = 2.0 * score_gap[:, None] * positive_vecs + 2.0 * penalty_coef * jnp.dot(user_vecs, item_gram, precision=lax.Precision.HIGHEST, preferred_element_type=jnp.float32)
    positive_grad = 2.0 * score_gap[:, None] * user_vecs
    per_history = jnp.broadcast_to((user_grad / HIST)[:, None, :], hist_rows.shape).reshape(-1, EMB)
    row_grad = 2.0 * penalty_coef * jnp.dot(item_table, user_gram, precision=lax.Precision.HIGHEST, preferred_element_type=jnp.float32)
    row_grad = row_grad.at[history_ids.reshape(-1)].add(per_history)
    row_grad = row_grad.at[positive_ids].add(positive_grad)
    new_state = adagrad_state + row_grad * row_grad
    new_table = item_table - step_size * row_grad / jnp.sqrt(new_state)
    return (new_table, new_state)
```

```python
import functools

import jax
import jax.numpy as jnp
from jax import lax
from jax.experimental import pallas as pl
from jax.experimental.pallas import tpu as pltpu
from jax.sharding import Mesh
from jax.sharding import PartitionSpec as P

DP_ROWS = ("dp_0", "dp_1", "rows_0", "rows_1")

penalty_weight = 10.0
step_size = 0.05

LANES = 128
BLOCK_ROWS = 264
CHAINS = 4

bf16 = jnp.bfloat16
f32 = jnp.float32
i32 = jnp.int32


def iota2(shape, dim):
    return lax.broadcasted_iota(i32, shape, dim)


def split2(x):
    hi = x.astype(bf16)
    lo = (x - hi.astype(f32)).astype(bf16)
    return hi, lo


def dot_f32(a, b):
    return jnp.dot(a, b, preferred_element_type=f32)


def dot_split(a, b):
    ah, al = split2(a)
    bh, bl = split2(b)
    return dot_f32(ah, bh) + (dot_f32(ah, bl) + dot_f32(al, bh))


def dot_split_t(a, b):
    dims = (((0,), (0,)), ((), ()))
    ah, al = split2(a)
    bh, bl = split2(b)
    dg = functools.partial(lax.dot_general, dimension_numbers=dims, preferred_element_type=f32)
    return dg(ah, bh) + (dg(ah, bl) + dg(al, bh))


def list_kernel(ids_c_ref, ids_r_ref, out_ref, code_ref, *, slots, rows_dev):
    sq = (LANES, LANES)
    lane = iota2(sq, 1)
    sub = iota2(sq, 0)
    lane_f = lane.astype(f32)
    one = jnp.ones(sq, f32)
    zero = jnp.zeros(sq, f32)
    lower = jnp.concatenate([jnp.where(sub > lane, one, zero), one], axis=0).astype(bf16)
    ones = one.astype(bf16)
    users = iota2((1, LANES), 1)
    carry = jnp.zeros(sq, f32)
    acc = jnp.zeros((3 * LANES, LANES), f32)
    for h in range(slots):
        owner_c = ids_c_ref[:, h : h + 1] // rows_dev
        member = owner_c == lane
        counts = dot_f32(lower, jnp.where(member, one, zero).astype(bf16))
        mine = jnp.where(member, counts[:LANES] + carry, zero).astype(bf16)
        rank = dot_f32(mine, ones)
        place = jnp.where(rank == lane_f, one, zero).astype(bf16)
        ids = ids_r_ref[h : h + 1, :]
        local = ids % rows_dev
        at_owner = ids // rows_dev == sub
        high = (local // 64 + 1).astype(f32)
        low = (local % 64).astype(f32)
        code = (users + (LANES if h == slots - 1 else 0)).astype(f32)
        vals = jnp.concatenate(
            [
                jnp.where(at_owner, jnp.broadcast_to(high, sq), zero),
                jnp.where(at_owner, jnp.broadcast_to(low, sq), zero),
                jnp.where(at_owner, jnp.broadcast_to(code, sq), zero),
            ],
            axis=0,
        ).astype(bf16)
        acc = acc + dot_f32(vals, place)
        carry = carry + counts[LANES:]
    high = acc[:LANES].astype(i32)
    low = acc[LANES : 2 * LANES].astype(i32)
    code = acc[2 * LANES :].astype(i32)
    present = high > 0
    out_ref[:, 0, :] = jnp.where(present, (high - 1) * 64 + low, rows_dev)
    code = jnp.where(present, code, -1)
    out_ref[:, 1, :] = code
    code_ref[...] = code


def request_lists(ids_c, ids_r, rows_dev, slots):
    return pl.pallas_call(
        functools.partial(list_kernel, slots=slots, rows_dev=rows_dev),
        out_shape=(
            jax.ShapeDtypeStruct((LANES, 2, LANES), i32),
            jax.ShapeDtypeStruct((LANES, LANES), i32),
        ),
        name="request_lists",
    )(ids_c, ids_r)


def pick_kernel(rows_ref, table_ref, out_ref, *, per_step):
    g = pl.program_id(0)

    def body(j, carry):
        for k in range(16):
            i = j * 16 + k
            row = rows_ref[g * (per_step // LANES) + j // 8, (j % 8) * 16 + k]
            out_ref[i] = table_ref[row]
        return carry

    lax.fori_loop(0, per_step // 16, body, 0)


def pick_rows(rows_idx, table, devices):
    rows_dev, width = table.shape
    total = devices * LANES
    per_step = 1024
    return pl.pallas_call(
        functools.partial(pick_kernel, per_step=per_step),
        grid_spec=pltpu.PrefetchScalarGridSpec(
            num_scalar_prefetch=1,
            grid=(total // per_step,),
            in_specs=[pl.BlockSpec((rows_dev, 1, width), lambda g, r: (0, 0, 0))],
            out_specs=pl.BlockSpec((per_step, 1, width), lambda g, r: (g, 0, 0)),
        ),
        out_shape=jax.ShapeDtypeStruct((total, 1, width), f32),
        compiler_params=pltpu.CompilerParams(vmem_limit_bytes=32 * 2**20),
        name="pick_rows",
    )(rows_idx, table.reshape(rows_dev, 1, width))


def user_kernel(code_ref, rows_ref, gram_ref, out_ref, acc_ref, *, hist_len, coef, owners):
    g = pl.program_id(0)

    @pl.when(g == 0)
    def _():
        acc_ref[...] = jnp.zeros_like(acc_ref)

    sub = iota2((2 * LANES, LANES), 0)
    one = jnp.ones((2 * LANES, LANES), f32)
    zero = jnp.zeros((2 * LANES, LANES), f32)
    total = acc_ref[...]
    for o in range(owners):
        weight = jnp.where(code_ref[o : o + 1, :] == sub, one, zero).astype(bf16)
        total = total + dot_f32(weight, jnp.concatenate(split2(rows_ref[o]), axis=1))
    acc_ref[...] = total

    @pl.when(g == pl.num_programs(0) - 1)
    def _():
        sums = acc_ref[:, :LANES] + acc_ref[:, LANES:]
        user = sums[:LANES] / hist_len
        positive = sums[LANES:]
        gap = jnp.sum(user * positive, axis=1, keepdims=True) - 1.0
        grad = 2.0 * gap * positive + 2.0 * coef * dot_split(user, gram_ref[...])
        out_ref[:LANES, :] = grad / hist_len
        out_ref[LANES : 2 * LANES, :] = user
        sq = (LANES, LANES)
        gap_row = jnp.sum(
            jnp.where(iota2(sq, 0) == iota2(sq, 1), jnp.broadcast_to(gap, sq), 0.0),
            axis=0,
            keepdims=True,
        )
        out_ref[2 * LANES :, :] = jnp.broadcast_to(gap_row, (8, LANES))


def user_block(codes, fetched, item_total, hist_len, coef):
    devices, capacity, width = fetched.shape
    owners = 8
    return pl.pallas_call(
        functools.partial(user_kernel, hist_len=hist_len, coef=coef, owners=owners),
        grid=(devices // owners,),
        in_specs=[
            pl.BlockSpec((owners, capacity), lambda g: (g, 0)),
            pl.BlockSpec((owners, capacity, width), lambda g: (g, 0, 0)),
            pl.BlockSpec((width, width), lambda g: (0, 0)),
        ],
        out_specs=pl.BlockSpec((BLOCK_ROWS, width), lambda g: (0, 0)),
        out_shape=jax.ShapeDtypeStruct((BLOCK_ROWS, width), f32),
        scratch_shapes=[pltpu.VMEM((2 * LANES, 2 * LANES), f32)],
        name="user_block",
    )(codes, fetched, item_total)


def update_kernel(
    idx_ref, blocks_ref, table_ref, state_ref, new_table_ref, new_state_ref,
    stage_ref, gram_ref, *acc_refs, sources, coef,
):
    g = pl.program_id(0)
    rows_dev = table_ref.shape[0]
    sq = (LANES, LANES)

    @pl.when(g == 0)
    def _():
        gram_ref[...] = jnp.zeros_like(gram_ref)
        for acc in acc_refs:
            acc[...] = jnp.zeros_like(acc)

    diagonal = iota2(sq, 0) == iota2(sq, 1)
    gram = gram_ref[...]
    for s in range(sources):
        user = blocks_ref[s, LANES : 2 * LANES, :]
        gap_row = blocks_ref[s, 2 * LANES : 2 * LANES + 1, :]
        gap = jnp.sum(
            jnp.where(diagonal, jnp.broadcast_to(gap_row, sq), 0.0), axis=1, keepdims=True
        )
        stage_ref[2 * LANES * s : 2 * LANES * s + LANES, :] = blocks_ref[s, :LANES, :]
        stage_ref[2 * LANES * s + LANES : 2 * LANES * (s + 1), :] = 2.0 * gap * user
        gram = gram + dot_split_t(user, user)
    gram_ref[...] = gram

    def body(j, carry):
        for k in range(8):
            packed = idx_ref[g * sources + j // 16, (j % 16) * 8 + k]
            row = packed // 2048
            src = packed % 2048
            acc = acc_refs[k % CHAINS]
            acc[pl.ds(row, 1), :] += stage_ref[pl.ds(src, 1), :]
        return carry

    lax.fori_loop(0, sources * LANES // 8, body, 0)

    @pl.when(g == pl.num_programs(0) - 1)
    def _():
        step = 512

        def finish(i, carry):
            at = pl.ds(pl.multiple_of(i * step, step), step)
            table = table_ref[at, :]
            grad = 2.0 * coef * dot_split(table, gram_ref[...])
            for acc in acc_refs:
                grad = grad + acc[at, :]
            new_state = state_ref[at, :] + grad * grad
            new_state_ref[at, :] = new_state
            new_table_ref[at, :] = table - step_size * grad / jnp.sqrt(new_state)
            return carry

        lax.fori_loop(0, rows_dev // step, finish, 0)


def update_rows(packed, blocks, table, state, coef):
    rows_dev, width = table.shape
    devices = packed.shape[0]
    sources = 8
    whole = pl.BlockSpec((rows_dev, width), lambda g, r: (0, 0))
    return pl.pallas_call(
        functools.partial(update_kernel, sources=sources, coef=coef),
        grid_spec=pltpu.PrefetchScalarGridSpec(
            num_scalar_prefetch=1,
            grid=(devices // sources,),
            in_specs=[
                pl.BlockSpec((sources, BLOCK_ROWS, width), lambda g, r: (g, 0, 0)),
                whole,
                whole,
            ],
            out_specs=[whole, whole],
            scratch_shapes=[
                pltpu.VMEM((sources * 2 * LANES, width), f32),
                pltpu.VMEM((width, width), f32),
            ]
            + [pltpu.VMEM((rows_dev + 8, width), f32)] * CHAINS,
        ),
        out_shape=(
            jax.ShapeDtypeStruct((rows_dev, width), f32),
            jax.ShapeDtypeStruct((rows_dev, width), f32),
        ),
        compiler_params=pltpu.CompilerParams(vmem_limit_bytes=48 * 2**20),
        name="update_rows",
    )(packed, blocks, table, state)


def shards(item_table, adagrad_state, history_ids, positive_ids):
    rows_dev, width = item_table.shape
    users_dev, hist_len = history_ids.shape
    devices = lax.axis_size(DP_ROWS)
    coef = penalty_weight / (rows_dev * devices)
    item_gram = jnp.dot(
        item_table.T,
        item_table,
        precision=lax.Precision.HIGHEST,
        preferred_element_type=f32,
    )
    item_total = lax.psum(item_gram, DP_ROWS)
    ids = jnp.concatenate([history_ids, positive_ids[:, None]], axis=1)
    lists, codes = request_lists(ids, ids.T, rows_dev, hist_len + 1)
    asked = lax.all_to_all(lists, DP_ROWS, split_axis=0, concat_axis=0, tiled=True)
    rows = asked[:, 0, :]
    source = jnp.maximum(asked[:, 1, :], 0)
    place = (jnp.arange(devices, dtype=i32) % 8 * (2 * LANES))[:, None]
    packed = rows * 2048 + place + source
    picked = pick_rows(jnp.where(rows < rows_dev, rows, 0), item_table, devices)
    fetched = lax.all_to_all(
        picked.reshape(devices, LANES, width), DP_ROWS, split_axis=0, concat_axis=0, tiled=True
    )
    block = user_block(codes, fetched, item_total, hist_len, coef)
    blocks = lax.all_gather(block, DP_ROWS)
    return update_rows(packed, blocks, item_table, adagrad_state, coef)


def solution(mesh):
    finer = Mesh(mesh.devices.reshape(4, 2, 4, 4), DP_ROWS)
    rows = P(DP_ROWS, None)
    return jax.shard_map(
        shards,
        mesh=finer,
        in_specs=(rows, rows, rows, P(DP_ROWS)),
        out_specs=(rows, rows),
        check_vma=False,
    )
```

```python
import functools

import jax
import jax.numpy as jnp
from jax import lax
from jax.experimental import pallas as pl
from jax.experimental.pallas import tpu as pltpu
from jax.sharding import Mesh
from jax.sharding import PartitionSpec as P

DP_ROWS = ("dp_0", "dp_1", "rows_0", "rows_1")

penalty_weight = 10.0
step_size = 0.05

LANES = 128
BLOCK_ROWS = 264
CHAINS = 8
ROW_BLOCK = 136

bf16 = jnp.bfloat16
f32 = jnp.float32
i32 = jnp.int32


def iota2(shape, dim):
    return lax.broadcasted_iota(i32, shape, dim)


def split2(x):
    hi = x.astype(bf16)
    lo = (x - hi.astype(f32)).astype(bf16)
    return hi, lo


def dot_f32(a, b):
    return jnp.dot(a, b, preferred_element_type=f32)


def dot_split(a, b):
    ah, al = split2(a)
    bh, bl = split2(b)
    return dot_f32(ah, bh) + (dot_f32(ah, bl) + dot_f32(al, bh))


def half_gram(a):
    hi, lo = split2(a)
    return lax.dot_general(
        hi,
        jnp.concatenate([hi, lo], axis=1),
        (((0,), (0,)), ((), ())),
        preferred_element_type=f32,
    )


def whole_gram(halves):
    cross = halves[:, LANES:]
    return halves[:, :LANES] + (cross + cross.T)


def list_kernel(ids_c_ref, ids_r_ref, gram_ref, out_ref, code_ref, *, slots, rows_dev):
    sq = (LANES, LANES)
    lane = iota2(sq, 1)
    sub = iota2(sq, 0)
    lane_f = lane.astype(f32)
    one = jnp.ones(sq, f32)
    zero = jnp.zeros(sq, f32)
    lower = jnp.concatenate([jnp.where(sub > lane, one, zero), one], axis=0).astype(bf16)
    ones = one.astype(bf16)
    users = iota2((1, LANES), 1)
    carry = jnp.zeros(sq, f32)
    acc = jnp.zeros((3 * LANES, LANES), f32)
    for h in range(slots):
        owner_c = ids_c_ref[:, h : h + 1] // rows_dev
        member = owner_c == lane
        counts = dot_f32(lower, jnp.where(member, one, zero).astype(bf16))
        mine = jnp.where(member, counts[:LANES] + carry, zero).astype(bf16)
        rank = dot_f32(mine, ones)
        place = jnp.where(rank == lane_f, one, zero).astype(bf16)
        ids = ids_r_ref[h : h + 1, :]
        local = ids % rows_dev
        at_owner = ids // rows_dev == sub
        high = (local // 64 + 1).astype(f32)
        low = (local % 64).astype(f32)
        code = (users + (LANES if h == slots - 1 else 0)).astype(f32)
        vals = jnp.concatenate(
            [
                jnp.where(at_owner, jnp.broadcast_to(high, sq), zero),
                jnp.where(at_owner, jnp.broadcast_to(low, sq), zero),
                jnp.where(at_owner, jnp.broadcast_to(code, sq), zero),
            ],
            axis=0,
        ).astype(bf16)
        acc = acc + dot_f32(vals, place)
        carry = carry + counts[LANES:]
    high = acc[:LANES].astype(i32)
    low = acc[LANES : 2 * LANES].astype(i32)
    code = acc[2 * LANES :].astype(i32)
    present = high > 0
    code = jnp.where(present, code, -1)
    out_ref[:, 0, :] = jnp.where(present, (high - 1) * 64 + low, rows_dev).astype(f32)
    out_ref[:, 1, :] = code.astype(f32)
    out_ref[:, 2, :] = gram_ref[...]
    out_ref[:, 3, :] = zero
    code_ref[...] = code


def request_lists(ids_c, ids_r, gram, rows_dev, slots):
    return pl.pallas_call(
        functools.partial(list_kernel, slots=slots, rows_dev=rows_dev),
        out_shape=(
            jax.ShapeDtypeStruct((LANES, 4, LANES), f32),
            jax.ShapeDtypeStruct((LANES, LANES), i32),
        ),
        name="request_lists",
    )(ids_c, ids_r, gram)


def pick_kernel(rows_ref, table_ref, total_ref, out_ref, *, dests):
    base = pl.program_id(0) * (dests * LANES)
    unroll = 64

    for d in range(dests):

        def body(j, carry, d=d):
            at = j * unroll
            picked = [
                table_ref[rows_ref[base + (d * LANES + at + k)]] for k in range(unroll)
            ]
            for k in range(unroll):
                out_ref[d * ROW_BLOCK + at + k] = picked[k]
            return carry

        lax.fori_loop(0, LANES // unroll, body, 0)
        for k in range(LANES, ROW_BLOCK):
            out_ref[d * ROW_BLOCK + k] = total_ref[0]


def pick_rows(rows_idx, table, total_row, devices):
    rows_dev, width = table.shape
    dests = 8
    return pl.pallas_call(
        functools.partial(pick_kernel, dests=dests),
        grid_spec=pltpu.PrefetchScalarGridSpec(
            num_scalar_prefetch=1,
            grid=(devices // dests,),
            in_specs=[
                pl.BlockSpec((rows_dev, 1, width), lambda g, r: (0, 0, 0)),
                pl.BlockSpec((1, 1, width), lambda g, r: (0, 0, 0)),
            ],
            out_specs=pl.BlockSpec((dests * ROW_BLOCK, 1, width), lambda g, r: (g, 0, 0)),
        ),
        out_shape=jax.ShapeDtypeStruct((devices * ROW_BLOCK, 1, width), f32),
        compiler_params=pltpu.CompilerParams(vmem_limit_bytes=32 * 2**20),
        name="pick_rows",
    )(rows_idx, table.reshape(rows_dev, 1, width), total_row.reshape(1, 1, width))


def user_kernel(code_ref, rows_ref, out_ref, acc_ref, gram_ref, *, hist_len, coef, owners):
    g = pl.program_id(0)

    @pl.when(g == 0)
    def _():
        acc_ref[...] = jnp.zeros_like(acc_ref)

    sub = iota2((2 * LANES, LANES), 0)
    one = jnp.ones((2 * LANES, LANES), f32)
    zero = jnp.zeros((2 * LANES, LANES), f32)
    total = acc_ref[...]
    for o in range(owners):
        weight = jnp.where(code_ref[o : o + 1, :] == sub, one, zero).astype(bf16)
        rows = rows_ref[o, :LANES, :]
        total = total + dot_f32(weight, jnp.concatenate(split2(rows), axis=1))
        gram_ref[pl.ds(g * owners + o, 1), :] = rows_ref[o, LANES : LANES + 1, :]
    acc_ref[...] = total

    @pl.when(g == pl.num_programs(0) - 1)
    def _():
        sums = acc_ref[:, :LANES] + acc_ref[:, LANES:]
        user = sums[:LANES] / hist_len
        positive = sums[LANES:]
        gap = jnp.sum(user * positive, axis=1, keepdims=True) - 1.0
        grad = 2.0 * gap * positive + 2.0 * coef * dot_split(user, gram_ref[...])
        out_ref[:LANES, :] = grad / hist_len
        out_ref[LANES : 2 * LANES, :] = user
        sq = (LANES, LANES)
        gap_row = jnp.sum(
            jnp.where(iota2(sq, 0) == iota2(sq, 1), jnp.broadcast_to(gap, sq), 0.0),
            axis=0,
            keepdims=True,
        )
        out_ref[2 * LANES :, :] = jnp.broadcast_to(gap_row, (8, LANES))


def user_block(codes, fetched, hist_len, coef):
    devices, _, width = fetched.shape
    owners = 8
    return pl.pallas_call(
        functools.partial(user_kernel, hist_len=hist_len, coef=coef, owners=owners),
        grid=(devices // owners,),
        in_specs=[
            pl.BlockSpec((owners, LANES), lambda g: (g, 0)),
            pl.BlockSpec((owners, ROW_BLOCK, width), lambda g: (g, 0, 0)),
        ],
        out_specs=pl.BlockSpec((BLOCK_ROWS, width), lambda g: (0, 0)),
        out_shape=jax.ShapeDtypeStruct((BLOCK_ROWS, width), f32),
        scratch_shapes=[pltpu.VMEM((2 * LANES, 2 * LANES), f32), pltpu.VMEM((width, width), f32)],
        name="user_block",
    )(codes, fetched)


def update_kernel(
    row_idx_ref, src_idx_ref, blocks_ref, table_ref, state_ref, new_table_ref, new_state_ref,
    stage_ref, gram_ref, *acc_refs, sources, coef,
):
    g = pl.program_id(0)
    rows_dev = table_ref.shape[0]
    sq = (LANES, LANES)

    @pl.when(g == 0)
    def _():
        gram_ref[...] = jnp.zeros_like(gram_ref)
        for acc in acc_refs:
            acc[...] = jnp.zeros_like(acc)

    diagonal = iota2(sq, 0) == iota2(sq, 1)
    users = []
    for s in range(sources):
        user = blocks_ref[s, LANES : 2 * LANES, :]
        gap_row = blocks_ref[s, 2 * LANES : 2 * LANES + 1, :]
        gap = jnp.sum(
            jnp.where(diagonal, jnp.broadcast_to(gap_row, sq), 0.0), axis=1, keepdims=True
        )
        stage_ref[2 * LANES * s : 2 * LANES * s + LANES, :] = blocks_ref[s, :LANES, :]
        stage_ref[2 * LANES * s + LANES : 2 * LANES * (s + 1), :] = 2.0 * gap * user
        users.append(user)
    gram_ref[...] += half_gram(jnp.concatenate(users, axis=0))

    base = g * (sources * LANES)
    unroll = 16

    def body(j, carry):
        for at in range(0, unroll, CHAINS):
            first = base + j * unroll + at
            rows = [row_idx_ref[first + k] for k in range(CHAINS)]
            srcs = [src_idx_ref[first + k] for k in range(CHAINS)]
            grads = [stage_ref[pl.ds(srcs[k], 1), :] for k in range(CHAINS)]
            sums = [acc_refs[k][pl.ds(rows[k], 1), :] + grads[k] for k in range(CHAINS)]
            for k in range(CHAINS):
                acc_refs[k][pl.ds(rows[k], 1), :] = sums[k]
        return carry

    lax.fori_loop(0, sources * LANES // unroll, body, 0)

    @pl.when(g == pl.num_programs(0) - 1)
    def _():
        step = 512
        gram = whole_gram(gram_ref[...])

        def finish(i, carry):
            at = pl.ds(pl.multiple_of(i * step, step), step)
            table = table_ref[at, :]
            grad = 2.0 * coef * dot_split(table, gram)
            for acc in acc_refs:
                grad = grad + acc[at, :]
            new_state = state_ref[at, :] + grad * grad
            new_state_ref[at, :] = new_state
            new_table_ref[at, :] = table - step_size * grad / jnp.sqrt(new_state)
            return carry

        lax.fori_loop(0, rows_dev // step, finish, 0)


def update_rows(row_idx, src_idx, blocks, table, state, coef):
    rows_dev, width = table.shape
    devices = blocks.shape[0]
    sources = 8
    whole = pl.BlockSpec((rows_dev, width), lambda g, r, s: (0, 0))
    return pl.pallas_call(
        functools.partial(update_kernel, sources=sources, coef=coef),
        grid_spec=pltpu.PrefetchScalarGridSpec(
            num_scalar_prefetch=2,
            grid=(devices // sources,),
            in_specs=[
                pl.BlockSpec((sources, BLOCK_ROWS, width), lambda g, r, s: (g, 0, 0)),
                whole,
                whole,
            ],
            out_specs=[whole, whole],
            scratch_shapes=[
                pltpu.VMEM((sources * 2 * LANES, width), f32),
                pltpu.VMEM((width, 2 * width), f32),
            ]
            + [pltpu.VMEM((rows_dev + 8, width), f32)] * CHAINS,
        ),
        out_shape=(
            jax.ShapeDtypeStruct((rows_dev, width), f32),
            jax.ShapeDtypeStruct((rows_dev, width), f32),
        ),
        compiler_params=pltpu.CompilerParams(vmem_limit_bytes=48 * 2**20),
        name="update_rows",
    )(row_idx, src_idx, blocks, table, state)


def shards(item_table, adagrad_state, history_ids, positive_ids):
    rows_dev, width = item_table.shape
    users_dev, hist_len = history_ids.shape
    devices = lax.axis_size(DP_ROWS)
    coef = penalty_weight / (rows_dev * devices)
    item_gram = jnp.dot(
        item_table.T,
        item_table,
        precision=lax.Precision.HIGHEST,
        preferred_element_type=f32,
    )
    ids = jnp.concatenate([history_ids, positive_ids[:, None]], axis=1)
    lists, codes = request_lists(ids, ids.T, item_gram, rows_dev, hist_len + 1)
    asked = lax.all_to_all(lists, DP_ROWS, split_axis=0, concat_axis=0, tiled=True)
    rows = asked[:, 0, :].astype(i32).reshape(-1)
    code = asked[:, 1, :].astype(i32).reshape(-1)
    total_row = asked[:, 2, :].sum(axis=0)
    place = jnp.arange(devices * LANES, dtype=i32) // LANES % 8 * (2 * LANES)
    src_idx = place + jnp.maximum(code, 0)
    picked = pick_rows(jnp.where(rows < rows_dev, rows, 0), item_table, total_row, devices)
    fetched = lax.all_to_all(
        picked.reshape(devices, ROW_BLOCK, width),
        DP_ROWS,
        split_axis=0,
        concat_axis=0,
        tiled=True,
    )
    block = user_block(codes, fetched, hist_len, coef)
    blocks = lax.all_gather(block, DP_ROWS)
    return update_rows(rows, src_idx, blocks, item_table, adagrad_state, coef)


def solution(mesh):
    finer = Mesh(mesh.devices.reshape(4, 2, 4, 4), DP_ROWS)
    rows = P(DP_ROWS, None)
    return jax.shard_map(
        shards,
        mesh=finer,
        in_specs=(rows, rows, rows, P(DP_ROWS)),
        out_specs=(rows, rows),
        check_vma=False,
    )
```

```python
import functools

import jax
import jax.numpy as jnp
from jax import lax
from jax.experimental import pallas as pl
from jax.experimental.pallas import tpu as pltpu
from jax.sharding import Mesh
from jax.sharding import PartitionSpec as P

X, CORE, Z, Y = "x", "core", "z", "y"
DP_ROWS = (X, CORE, Z, Y)

penalty_weight = 10.0
step_size = 0.05

LANES = 128
BLOCK_ROWS = 264
CHAINS = 8
PARTS = ((0, 88), (88, 176), (176, 256))

bf16 = jnp.bfloat16
f32 = jnp.float32
i32 = jnp.int32


def iota2(shape, dim):
    return lax.broadcasted_iota(i32, shape, dim)


def split2(x):
    hi = x.astype(bf16)
    lo = (x - hi.astype(f32)).astype(bf16)
    return hi, lo


def dot_f32(a, b):
    return jnp.dot(a, b, preferred_element_type=f32)


def dot_split(a, b):
    ah, al = split2(a)
    bh, bl = split2(b)
    return dot_f32(ah, bh) + (dot_f32(ah, bl) + dot_f32(al, bh))


def half_gram(a):
    hi, lo = split2(a)
    return lax.dot_general(
        hi,
        jnp.concatenate([hi, lo], axis=1),
        (((0,), (0,)), ((), ())),
        preferred_element_type=f32,
    )


def whole_gram(halves):
    cross = halves[:, LANES:]
    return halves[:, :LANES] + (cross + cross.T)


def list_kernel(ids_c_ref, ids_r_ref, gram_ref, out_ref, *, slots, rows_dev):
    sq = (LANES, LANES)
    lane = iota2(sq, 1)
    sub = iota2(sq, 0)
    lane_f = lane.astype(f32)
    one = jnp.ones(sq, f32)
    zero = jnp.zeros(sq, f32)
    lower = jnp.concatenate([jnp.where(sub > lane, one, zero), one], axis=0).astype(bf16)
    ones = one.astype(bf16)
    users = iota2((1, LANES), 1)
    carry = jnp.zeros(sq, f32)
    acc = jnp.zeros((3 * LANES, LANES), f32)
    for h in range(slots):
        owner_c = ids_c_ref[:, h : h + 1] // rows_dev
        member = owner_c == lane
        counts = dot_f32(lower, jnp.where(member, one, zero).astype(bf16))
        mine = jnp.where(member, counts[:LANES] + carry, zero).astype(bf16)
        rank = dot_f32(mine, ones)
        place = jnp.where(rank == lane_f, one, zero).astype(bf16)
        ids = ids_r_ref[h : h + 1, :]
        local = ids % rows_dev
        at_owner = ids // rows_dev == sub
        high = (local // 64 + 1).astype(f32)
        low = (local % 64).astype(f32)
        code = (users + (LANES if h == slots - 1 else 0)).astype(f32)
        vals = jnp.concatenate(
            [
                jnp.where(at_owner, jnp.broadcast_to(high, sq), zero),
                jnp.where(at_owner, jnp.broadcast_to(low, sq), zero),
                jnp.where(at_owner, jnp.broadcast_to(code, sq), zero),
            ],
            axis=0,
        ).astype(bf16)
        acc = acc + dot_f32(vals, place)
        carry = carry + counts[LANES:]
    high = acc[:LANES].astype(i32)
    low = acc[LANES : 2 * LANES].astype(i32)
    code = acc[2 * LANES :].astype(i32)
    present = high > 0
    code = jnp.where(present, code, -1)
    out_ref[:, 0, :] = jnp.where(present, (high - 1) * 64 + low, rows_dev).astype(f32)
    out_ref[:, 1, :] = code.astype(f32)
    out_ref[:, 2, :] = gram_ref[...]
    out_ref[:, 3, :] = zero


def request_lists(ids_c, ids_r, gram, rows_dev, slots):
    return pl.pallas_call(
        functools.partial(list_kernel, slots=slots, rows_dev=rows_dev),
        out_shape=jax.ShapeDtypeStruct((LANES, 4, LANES), f32),
        name="request_lists",
    )(ids_c, ids_r, gram)


def partial_kernel(rows_ref, here_ref, table_ref, codes_ref, *refs, half, other_core):
    if other_core:
        (out_ref,) = refs[:1]
        scratch = refs[1:]
    else:
        from_ref = refs[0]
        outs = refs[1:11]
        scratch = refs[11:]
    picked_refs, block_refs = scratch[:4], scratch[4:]
    dx = pl.program_id(0)
    dz = pl.program_id(1)
    at_x = (here_ref[0] + (dx + 2 * half)) & 3
    at_core = here_ref[1] ^ 1 if other_core else here_ref[1]
    at_z = (here_ref[2] + dz) & 3
    code_of = iota2((2 * LANES, LANES), 0).astype(f32)
    one = jnp.ones((2 * LANES, LANES), f32)
    zero = jnp.zeros((2 * LANES, LANES), f32)
    unroll = 32
    for dy in range(4):
        at_y = (here_ref[3] + dy) & 3
        source = ((at_x * 2 + at_core) * 4 + at_z) * 4 + at_y
        base = source * LANES
        picked_ref = picked_refs[dy]
        for at in range(0, LANES, unroll):
            picked = [table_ref[pl.ds(rows_ref[base + (at + k)], 1), :] for k in range(unroll)]
            for k in range(unroll):
                picked_ref[at + k : at + k + 1, :] = picked[k]
        weight = jnp.where(codes_ref[pl.ds(source, 1), :] == code_of, one, zero).astype(bf16)
        block = dot_f32(
            jnp.concatenate([weight, weight], axis=1),
            jnp.concatenate(split2(picked_ref[...]), axis=0),
        )
        if other_core:
            out_ref[0, 0, dy] = block
        else:
            block_refs[dy][...] = block + from_ref[0, 0, dy]
    if other_core:
        return
    (a0, a1), (b0, b1), (c0, c1) = PARTS
    for i in range(2):

        @pl.when(dx == i)
        def _(i=i):
            for dy in range(4):
                outs[i][dz, dy] = block_refs[dy][a0:a1, :]

    for j in range(4):

        @pl.when(dz == j)
        def _(j=j):
            for dy in range(4):
                outs[2 + j][dy, dx] = block_refs[dy][b0:b1, :]

    for dy in range(4):
        outs[6 + dy][dx, dz] = block_refs[dy][c0:c1, :]


def partial_sums(rows_idx, here, table, codes, half, received=None):
    rows_dev, width = table.shape
    other_core = received is None
    blocks = pl.BlockSpec((1, 1, 4, 2 * LANES, width), lambda dx, dz, r, h: (dx, dz, 0, 0, 0))

    def whole(shape):
        return pl.BlockSpec(shape, lambda dx, dz, r, h: (0,) * len(shape))

    in_specs = [whole((rows_dev, width)), whole(codes.shape)]
    operands = (rows_idx, here, table, codes)
    scratch = [pltpu.VMEM((LANES, width), f32)] * 4
    if other_core:
        shapes = [(2, 4, 4, 2 * LANES, width)]
        out_specs = [blocks]
    else:
        in_specs.append(blocks)
        operands += (received,)
        la, lb, lc = (end - start for start, end in PARTS)
        shapes = [(4, 4, la, width)] * 2 + [(4, 2, lb, width)] * 4 + [(2, 4, lc, width)] * 4
        out_specs = [whole(shape) for shape in shapes]
        scratch = scratch + [pltpu.VMEM((2 * LANES, width), f32)] * 4
    return pl.pallas_call(
        functools.partial(partial_kernel, half=half, other_core=other_core),
        grid_spec=pltpu.PrefetchScalarGridSpec(
            num_scalar_prefetch=2,
            grid=(2, 4),
            in_specs=in_specs,
            out_specs=out_specs,
            scratch_shapes=scratch,
        ),
        out_shape=[jax.ShapeDtypeStruct(shape, f32) for shape in shapes],
        compiler_params=pltpu.CompilerParams(vmem_limit_bytes=40 * 2**20),
        name="partial_other" if other_core else "partial_own",
    )(*operands)


def split_sum_kernel(*refs, halves):
    at = 0
    outs = refs[4 * sum(halves) :]
    for part, n in enumerate(halves):
        pieces = [refs[at + d * n : at + (d + 1) * n] for d in range(4)]
        at += 4 * n
        for i in range(4):
            out_ref = outs[4 * part + i]
            if n == 1:
                spots = [(0, i, slice(None))]
            elif pieces[0][0].shape[0] == 2:
                spots = [(i // 2, i % 2, slice(None))]
            else:
                spots = [(half, i, slice(2 * half, 2 * half + 2)) for half in range(2)]
            for half, place, into in spots:
                total = pieces[0][half][place] + pieces[1][half][place]
                total = total + (pieces[2][half][place] + pieces[3][half][place])
                out_ref[into] = total


def split_sums(parts, name):
    operands = [half for part in parts for pieces in part for half in pieces]
    out_shape = [
        jax.ShapeDtypeStruct((4,) * (part[0][0].ndim - 3) + part[0][0].shape[-2:], f32)
        for part in parts
        for _ in range(4)
    ]
    outs = pl.pallas_call(
        functools.partial(split_sum_kernel, halves=tuple(len(part[0]) for part in parts)),
        out_shape=out_shape,
        compiler_params=pltpu.CompilerParams(vmem_limit_bytes=40 * 2**20),
        name=name,
    )(*operands)
    return [outs[4 * part : 4 * part + 4] for part in range(3)]


def shifted(array, axis, by):
    return lax.ppermute(array, axis, [(i, (i + by) % 4) for i in range(4)])


def to_sources(rows_idx, here, table, codes):
    swap = [(0, 1), (1, 0)]
    received = []
    for half in range(2):
        (mine,) = partial_sums(rows_idx, here, table, codes, half)
        received.append(lax.ppermute(mine, CORE, swap))
    first, second, third = [[], [], [], []], [[], [], [], []], [[], [], [], []]
    for half in range(2):
        outs = partial_sums(rows_idx, here, table, codes, half, received[half])
        for i in range(2):
            d = 2 * half + i
            first[d].append(outs[i] if d == 0 else shifted(outs[i], X, d))
        for d in range(4):
            second[d].append(outs[2 + d] if d == 0 else shifted(outs[2 + d], Z, d))
            third[d].append(outs[6 + d] if d == 0 else shifted(outs[6 + d], Y, d))
    first, second, third = split_sums([first, second, third], "sum_stage_1")
    moved = [
        [[piece if d == 0 else shifted(piece, axis, d)] for d, piece in enumerate(part)]
        for part, axis in ((first, Z), (second, Y), (third, X))
    ]
    first, second, third = split_sums(moved, "sum_stage_2")
    return [
        [piece if d == 0 else shifted(piece, axis, d) for d, piece in enumerate(part)]
        for part, axis in ((first, Y), (second, X), (third, Z))
    ]


def user_kernel(*refs, hist_len):
    total_ref, out_ref = refs[12:]
    sums = []
    for part in range(3):
        piece = refs[4 * part : 4 * part + 4]
        sums.append((piece[0][...] + piece[1][...]) + (piece[2][...] + piece[3][...]))
    sums = jnp.concatenate(sums, axis=0)
    user = sums[:LANES] / hist_len
    positive = sums[LANES:]
    gap = jnp.sum(user * positive, axis=1, keepdims=True) - 1.0
    sq = (LANES, LANES)
    gap_row = jnp.sum(
        jnp.where(iota2(sq, 0) == iota2(sq, 1), jnp.broadcast_to(gap, sq), 0.0),
        axis=0,
        keepdims=True,
    )
    out_ref[:LANES, :] = positive
    out_ref[LANES : 2 * LANES, :] = user
    tail = (8, LANES)
    out_ref[2 * LANES :, :] = jnp.where(
        iota2(tail, 0) == 0,
        jnp.broadcast_to(gap_row, tail),
        jnp.broadcast_to(total_ref[...], tail),
    )


def user_block(parts, total_row, hist_len):
    width = total_row.shape[-1]
    return pl.pallas_call(
        functools.partial(user_kernel, hist_len=hist_len),
        out_shape=jax.ShapeDtypeStruct((BLOCK_ROWS, width), f32),
        name="user_block",
    )(*[piece for part in parts for piece in part], total_row)


def update_kernel(
    row_idx_ref, src_idx_ref, blocks_ref, item_ref, table_ref, state_ref, new_table_ref, new_state_ref,
    stage_ref, gram_ref, *acc_refs, sources, coef, hist_len,
):
    g = pl.program_id(0)
    rows_dev = table_ref.shape[0]
    sq = (LANES, LANES)

    @pl.when(g == 0)
    def _():
        gram_ref[...] = jnp.zeros_like(gram_ref)
        for acc in acc_refs:
            acc[...] = jnp.zeros_like(acc)

    diagonal = iota2(sq, 0) == iota2(sq, 1)
    users = jnp.concatenate(
        [blocks_ref[s, LANES : 2 * LANES, :] for s in range(sources)], axis=0
    )
    pulls = dot_split(users, item_ref[...])
    for s in range(sources):
        user = blocks_ref[s, LANES : 2 * LANES, :]
        gap_row = blocks_ref[s, 2 * LANES : 2 * LANES + 1, :]
        gap = 2.0 * jnp.sum(
            jnp.where(diagonal, jnp.broadcast_to(gap_row, sq), 0.0), axis=1, keepdims=True
        )
        pull = pulls[LANES * s : LANES * (s + 1)]
        grad = gap * blocks_ref[s, :LANES, :] + 2.0 * coef * pull
        stage_ref[2 * LANES * s : 2 * LANES * s + LANES, :] = grad / hist_len
        stage_ref[2 * LANES * s + LANES : 2 * LANES * (s + 1), :] = gap * user
    gram_ref[...] += half_gram(users)

    base = g * (sources * LANES)
    unroll = 16

    def body(j, carry):
        for at in range(0, unroll, CHAINS):
            first = base + j * unroll + at
            rows = [row_idx_ref[first + k] for k in range(CHAINS)]
            srcs = [src_idx_ref[first + k] for k in range(CHAINS)]
            grads = [stage_ref[pl.ds(srcs[k], 1), :] for k in range(CHAINS)]
            sums = [acc_refs[k][pl.ds(rows[k], 1), :] + grads[k] for k in range(CHAINS)]
            for k in range(CHAINS):
                acc_refs[k][pl.ds(rows[k], 1), :] = sums[k]
        return carry

    lax.fori_loop(0, sources * LANES // unroll, body, 0)

    @pl.when(g == pl.num_programs(0) - 1)
    def _():
        step = 512
        gram = whole_gram(gram_ref[...])

        def finish(i, carry):
            at = pl.ds(pl.multiple_of(i * step, step), step)
            table = table_ref[at, :]
            grad = 2.0 * coef * dot_split(table, gram)
            for acc in acc_refs:
                grad = grad + acc[at, :]
            new_state = state_ref[at, :] + grad * grad
            new_state_ref[at, :] = new_state
            new_table_ref[at, :] = table - step_size * grad / jnp.sqrt(new_state)
            return carry

        lax.fori_loop(0, rows_dev // step, finish, 0)


def update_rows(row_idx, src_idx, blocks, item_total, table, state, coef, hist_len):
    rows_dev, width = table.shape
    devices = blocks.shape[0]
    sources = 8
    whole = pl.BlockSpec((rows_dev, width), lambda g, r, s: (0, 0))
    return pl.pallas_call(
        functools.partial(update_kernel, sources=sources, coef=coef, hist_len=hist_len),
        grid_spec=pltpu.PrefetchScalarGridSpec(
            num_scalar_prefetch=2,
            grid=(devices // sources,),
            in_specs=[
                pl.BlockSpec((sources, BLOCK_ROWS, width), lambda g, r, s: (g, 0, 0)),
                pl.BlockSpec((width, width), lambda g, r, s: (0, 0)),
                whole,
                whole,
            ],
            out_specs=[whole, whole],
            scratch_shapes=[
                pltpu.VMEM((sources * 2 * LANES, width), f32),
                pltpu.VMEM((width, 2 * width), f32),
            ]
            + [pltpu.VMEM((rows_dev + 8, width), f32)] * CHAINS,
        ),
        out_shape=(
            jax.ShapeDtypeStruct((rows_dev, width), f32),
            jax.ShapeDtypeStruct((rows_dev, width), f32),
        ),
        compiler_params=pltpu.CompilerParams(vmem_limit_bytes=48 * 2**20),
        name="update_rows",
    )(row_idx, src_idx, blocks, item_total, table, state)


def shards(item_table, adagrad_state, history_ids, positive_ids):
    rows_dev, width = item_table.shape
    users_dev, hist_len = history_ids.shape
    devices = lax.axis_size(DP_ROWS)
    coef = penalty_weight / (rows_dev * devices)
    item_gram = jnp.dot(
        item_table.T,
        item_table,
        precision=lax.Precision.HIGHEST,
        preferred_element_type=f32,
    )
    ids = jnp.concatenate([history_ids, positive_ids[:, None]], axis=1)
    lists = request_lists(ids, ids.T, item_gram, rows_dev, hist_len + 1)
    asked = lax.all_to_all(lists, DP_ROWS, split_axis=0, concat_axis=0, tiled=True)
    rows = asked[:, 0, :].astype(i32).reshape(-1)
    codes = asked[:, 1, :]
    total_row = asked[:, 2, :].sum(axis=0, keepdims=True)
    place = jnp.arange(devices * LANES, dtype=i32) // LANES % 8 * (2 * LANES)
    src_idx = place + jnp.maximum(codes.astype(i32).reshape(-1), 0)
    here = jnp.stack([lax.axis_index(axis) for axis in DP_ROWS]).astype(i32)
    parts = to_sources(jnp.where(rows < rows_dev, rows, 0), here, item_table, codes)
    block = user_block(parts, total_row, hist_len)
    blocks = lax.all_gather(block, DP_ROWS)
    item_total = blocks[:, 2 * LANES + 1, :]
    return update_rows(
        rows, src_idx, blocks, item_total, item_table, adagrad_state, coef, hist_len
    )


def solution(mesh):
    finer = Mesh(mesh.devices.reshape(4, 2, 4, 4), DP_ROWS)
    rows = P(DP_ROWS, None)
    return jax.shard_map(
        shards,
        mesh=finer,
        in_specs=(rows, rows, rows, P(DP_ROWS)),
        out_specs=(rows, rows),
        check_vma=False,
    )
```

```python
import functools

import jax
import jax.numpy as jnp
from jax import lax
from jax.experimental import pallas as pl
from jax.experimental.pallas import tpu as pltpu
from jax.sharding import Mesh
from jax.sharding import PartitionSpec as P

X, CORE, Z, Y = "x", "core", "z", "y"
DP_ROWS = (X, CORE, Z, Y)

penalty_weight = 10.0
step_size = 0.05

LANES = 128
BLOCK_ROWS = 264
IN_FLIGHT = 5
CHAINS = 8
PART_ROWS = 88

bf16 = jnp.bfloat16
f32 = jnp.float32
i32 = jnp.int32


def iota2(shape, dim):
    return lax.broadcasted_iota(i32, shape, dim)


def split2(x):
    hi = x.astype(bf16)
    lo = (x - hi.astype(f32)).astype(bf16)
    return hi, lo


def dot_f32(a, b):
    return jnp.dot(a, b, preferred_element_type=f32)


def dot_split(a, b):
    ah, al = split2(a)
    bh, bl = split2(b)
    return dot_f32(ah, bh) + (dot_f32(ah, bl) + dot_f32(al, bh))


def half_gram(a):
    hi, lo = split2(a)
    return lax.dot_general(
        hi,
        jnp.concatenate([hi, lo], axis=1),
        (((0,), (0,)), ((), ())),
        preferred_element_type=f32,
    )


def whole_gram(halves):
    cross = halves[:, LANES:]
    return halves[:, :LANES] + (cross + cross.T)


def list_kernel(history_ref, positive_ref, out_ref, *, slots, rows_dev):
    ids_r = jnp.concatenate(
        [history_ref[...], positive_ref[...], jnp.zeros((LANES - slots, LANES), i32)], axis=0
    )
    ids_c = ids_r.T
    sq = (LANES, LANES)
    lane = iota2(sq, 1)
    sub = iota2(sq, 0)
    lane_f = lane.astype(f32)
    one = jnp.ones(sq, f32)
    zero = jnp.zeros(sq, f32)
    lower = jnp.concatenate([jnp.where(sub > lane, one, zero), one], axis=0).astype(bf16)
    ones = one.astype(bf16)
    users = iota2((1, LANES), 1)
    carry = jnp.zeros(sq, f32)
    acc = jnp.zeros((3 * LANES, LANES), f32)
    for h in range(slots):
        owner_c = ids_c[:, h : h + 1] // rows_dev
        member = owner_c == lane
        counts = dot_f32(lower, jnp.where(member, one, zero).astype(bf16))
        mine = jnp.where(member, counts[:LANES] + carry, zero).astype(bf16)
        rank = dot_f32(mine, ones)
        place = jnp.where(rank == lane_f, one, zero).astype(bf16)
        ids = ids_r[h : h + 1, :]
        local = ids % rows_dev
        at_owner = ids // rows_dev == sub
        high = (local // 64 + 1).astype(f32)
        low = (local % 64).astype(f32)
        code = (users + (LANES if h == slots - 1 else 0)).astype(f32)
        vals = jnp.concatenate(
            [
                jnp.where(at_owner, jnp.broadcast_to(high, sq), zero),
                jnp.where(at_owner, jnp.broadcast_to(low, sq), zero),
                jnp.where(at_owner, jnp.broadcast_to(code, sq), zero),
            ],
            axis=0,
        ).astype(bf16)
        acc = acc + dot_f32(vals, place)
        carry = carry + counts[LANES:]
    high = acc[:LANES].astype(i32)
    low = acc[LANES : 2 * LANES].astype(i32)
    code = acc[2 * LANES :].astype(i32)
    present = high > 0
    code = jnp.where(present, code, -1)
    out_ref[:, 0, :] = jnp.where(present, (high - 1) * 64 + low, rows_dev).astype(f32)
    out_ref[:, 1, :] = code.astype(f32)


def request_lists(history_ids, positive_ids, rows_dev):
    users, hist_len = history_ids.shape
    return pl.pallas_call(
        functools.partial(list_kernel, slots=hist_len + 1, rows_dev=rows_dev),
        out_shape=jax.ShapeDtypeStruct((LANES, 2, LANES), f32),
        name="request_lists",
    )(history_ids.T, positive_ids.reshape(1, users))


def partial_kernel(rows_ref, here_ref, table_ref, codes_ref, gram_ref, *refs, half, other_core):
    if other_core:
        out_ref = refs[0]
        scratch = refs[1:]
    else:
        from_ref = refs[0]
        earlier = refs[1 : 1 + 8 * half]
        outs = refs[1 + 8 * half : 11 + 8 * half]
        scratch = refs[11 + 8 * half :]
    picked_refs, block_refs = scratch[:4], scratch[4:]
    dx = pl.program_id(0)
    dz = pl.program_id(1)
    at_x = (here_ref[0] + (dx + 2 * half)) & 3
    at_core = here_ref[1] ^ 1 if other_core else here_ref[1]
    at_z = (here_ref[2] + dz) & 3
    code_of = iota2((2 * LANES, LANES), 0).astype(f32)
    one = jnp.ones((2 * LANES, LANES), f32)
    zero = jnp.zeros((2 * LANES, LANES), f32)
    unroll = 32
    for dy in range(4):
        at_y = (here_ref[3] + dy) & 3
        source = ((at_x * 2 + at_core) * 4 + at_z) * 4 + at_y
        base = source * LANES
        picked_ref = picked_refs[dy]
        for at in range(0, LANES, unroll):
            picked = [table_ref[pl.ds(rows_ref[base + (at + k)], 1), :] for k in range(unroll)]
            for k in range(unroll):
                picked_ref[at + k : at + k + 1, :] = picked[k]
        weight = jnp.where(codes_ref[pl.ds(source, 1), :] == code_of, one, zero).astype(bf16)
        block = dot_f32(
            jnp.concatenate([weight, weight], axis=1),
            jnp.concatenate(split2(picked_ref[...]), axis=0),
        )
        gram = jnp.broadcast_to(gram_ref[pl.ds(source, 1), :], (8, LANES))
        if other_core:
            out_ref[0, 0, dy, : 2 * LANES, :] = block
            out_ref[0, 0, dy, 2 * LANES :, :] = gram
        else:
            block_refs[dy][: 2 * LANES, :] = block + from_ref[0, 0, dy, : 2 * LANES, :]
            block_refs[dy][2 * LANES :, :] = gram + from_ref[0, 0, dy, 2 * LANES :, :]
    if other_core:
        return
    n = PART_ROWS
    for i in range(2):

        @pl.when(dx == i)
        def _(i=i):
            for dy in range(4):
                outs[i][dz, dy] = block_refs[dy][:n, :]

    for j in range(4):

        @pl.when(dz == j)
        def _(j=j):
            for dy in range(4):
                outs[2 + j][dy, dx + 2 * half] = block_refs[dy][n : 2 * n, :]

    for dy in range(4):
        outs[6 + dy][dx + 2 * half, dz] = block_refs[dy][2 * n :, :]

    if half:

        @pl.when((dx == 0) & (dz == 0))
        def _():
            for j in range(4):
                for k in range(4):
                    for m in range(2):
                        outs[2 + j][k, m] = earlier[j][k, m]
                        outs[6 + j][m, k] = earlier[4 + j][m, k]


def partial_sums(rows_idx, here, table, codes, gram, half, received=None, earlier=()):
    rows_dev, width = table.shape
    other_core = received is None
    blocks = pl.BlockSpec((1, 1, 4, BLOCK_ROWS, width), lambda dx, dz, r, h: (dx, dz, 0, 0, 0))

    def whole(shape):
        return pl.BlockSpec(shape, lambda dx, dz, r, h: (0,) * len(shape))

    in_specs = [whole((rows_dev, width)), whole(codes.shape), whole(gram.shape)]
    operands = (rows_idx, here, table, codes, gram)
    scratch = [pltpu.VMEM((LANES, width), f32)] * 4
    if other_core:
        shapes = [(2, 4, 4, BLOCK_ROWS, width)]
        out_specs = [blocks]
    else:
        in_specs += [blocks] + [whole(piece.shape) for piece in earlier]
        operands += (received, *earlier)
        end = (PART_ROWS, width)
        shapes = [(4, 4) + end] * 2
        if half:
            shapes += [(4, 4) + end] * 8
        else:
            shapes += [(4, 2) + end] * 4 + [(2, 4) + end] * 4
        out_specs = [whole(shape) for shape in shapes]
        scratch = scratch + [pltpu.VMEM((BLOCK_ROWS, width), f32)] * 4
    return pl.pallas_call(
        functools.partial(partial_kernel, half=half, other_core=other_core),
        grid_spec=pltpu.PrefetchScalarGridSpec(
            num_scalar_prefetch=2,
            grid=(2, 4),
            in_specs=in_specs,
            out_specs=out_specs,
            scratch_shapes=scratch,
        ),
        out_shape=[jax.ShapeDtypeStruct(shape, f32) for shape in shapes],
        compiler_params=pltpu.CompilerParams(vmem_limit_bytes=40 * 2**20),
        name="partial_other" if other_core else "partial_own",
    )(*operands)


def split_sum_kernel(*refs):
    outs = refs[12:]
    for part in range(3):
        pieces = refs[4 * part : 4 * part + 4]
        for i in range(4):
            total = (pieces[0][i] + pieces[1][i]) + (pieces[2][i] + pieces[3][i])
            outs[4 * part + i][...] = total


def split_sums(parts, name):
    operands = [piece for part in parts for piece in part]
    outs = pl.pallas_call(
        split_sum_kernel,
        out_shape=[jax.ShapeDtypeStruct(operands[0].shape[1:], f32)] * 12,
        compiler_params=pltpu.CompilerParams(vmem_limit_bytes=40 * 2**20),
        name=name,
    )(*operands)
    return [outs[4 * part : 4 * part + 4] for part in range(3)]


def shifted(array, axis, by):
    return lax.ppermute(array, axis, [(i, (i + by) % 4) for i in range(4)])


def moved(parts, axes):
    order = [(part, d) for d in (1, 3, 2) for part in range(3)]
    results = [[part[0], None, None, None] for part in parts]
    done = []
    for k, (part, d) in enumerate(order):
        piece = parts[part][d]
        if k >= IN_FLIGHT:
            piece, _ = lax.optimization_barrier((piece, done[k - IN_FLIGHT]))
        done.append(shifted(piece, axes[part], d))
        results[part][d] = done[-1]
    return results


def to_sources(rows_idx, here, table, codes, gram):
    swap = [(0, 1), (1, 0)]
    call = functools.partial(partial_sums, rows_idx, here, table, codes, gram)
    received = [lax.ppermute(call(half)[0], CORE, swap) for half in range(2)]
    early = call(0, received[0])
    late = call(1, received[1], early[2:])
    parts = [[early[0], early[1], late[0], late[1]], late[2:6], late[6:10]]
    parts = split_sums(moved(parts, (X, Z, Y)), "sum_stage_1")
    parts = split_sums(moved(parts, (Z, Y, X)), "sum_stage_2")
    return moved(parts, (Y, X, Z))


def user_kernel(*refs, hist_len):
    out_ref = refs[12]
    sums = []
    for part in range(3):
        piece = refs[4 * part : 4 * part + 4]
        sums.append((piece[0][...] + piece[1][...]) + (piece[2][...] + piece[3][...]))
    sums = jnp.concatenate(sums, axis=0)
    user = sums[:LANES] / hist_len
    positive = sums[LANES : 2 * LANES]
    gap = jnp.sum(user * positive, axis=1, keepdims=True) - 1.0
    sq = (LANES, LANES)
    gap_row = jnp.sum(
        jnp.where(iota2(sq, 0) == iota2(sq, 1), jnp.broadcast_to(gap, sq), 0.0),
        axis=0,
        keepdims=True,
    )
    out_ref[:LANES, :] = positive
    out_ref[LANES : 2 * LANES, :] = user
    tail = (8, LANES)
    out_ref[2 * LANES :, :] = jnp.where(
        iota2(tail, 0) == 0,
        jnp.broadcast_to(gap_row, tail),
        sums[2 * LANES :],
    )


def user_block(parts, hist_len):
    pieces = [piece for part in parts for piece in part]
    return pl.pallas_call(
        functools.partial(user_kernel, hist_len=hist_len),
        out_shape=jax.ShapeDtypeStruct((BLOCK_ROWS, pieces[0].shape[-1]), f32),
        name="user_block",
    )(*pieces)


def update_kernel(
    row_idx_ref, src_idx_ref, blocks_ref, item_ref, table_ref, state_ref, new_table_ref, new_state_ref,
    stage_ref, gram_ref, *acc_refs, sources, coef, hist_len,
):
    g = pl.program_id(0)
    rows_dev = table_ref.shape[0]
    sq = (LANES, LANES)

    @pl.when(g == 0)
    def _():
        gram_ref[...] = jnp.zeros_like(gram_ref)
        for acc in acc_refs:
            acc[...] = jnp.zeros_like(acc)

    diagonal = iota2(sq, 0) == iota2(sq, 1)
    users = jnp.concatenate(
        [blocks_ref[s, LANES : 2 * LANES, :] for s in range(sources)], axis=0
    )
    pulls = dot_split(users, item_ref[...])
    for s in range(sources):
        user = blocks_ref[s, LANES : 2 * LANES, :]
        gap_row = blocks_ref[s, 2 * LANES : 2 * LANES + 1, :]
        gap = 2.0 * jnp.sum(
            jnp.where(diagonal, jnp.broadcast_to(gap_row, sq), 0.0), axis=1, keepdims=True
        )
        pull = pulls[LANES * s : LANES * (s + 1)]
        grad = gap * blocks_ref[s, :LANES, :] + 2.0 * coef * pull
        stage_ref[2 * LANES * s : 2 * LANES * s + LANES, :] = grad / hist_len
        stage_ref[2 * LANES * s + LANES : 2 * LANES * (s + 1), :] = gap * user
    gram_ref[...] += half_gram(users)

    base = g * (sources * LANES)
    unroll = 16

    def body(j, carry):
        for at in range(0, unroll, CHAINS):
            first = base + j * unroll + at
            rows = [row_idx_ref[first + k] for k in range(CHAINS)]
            srcs = [src_idx_ref[first + k] for k in range(CHAINS)]
            grads = [stage_ref[pl.ds(srcs[k], 1), :] for k in range(CHAINS)]
            sums = [acc_refs[k][pl.ds(rows[k], 1), :] + grads[k] for k in range(CHAINS)]
            for k in range(CHAINS):
                acc_refs[k][pl.ds(rows[k], 1), :] = sums[k]
        return carry

    lax.fori_loop(0, sources * LANES // unroll, body, 0)

    @pl.when(g == pl.num_programs(0) - 1)
    def _():
        step = 512
        gram = whole_gram(gram_ref[...])

        def finish(i, carry):
            at = pl.ds(pl.multiple_of(i * step, step), step)
            table = table_ref[at, :]
            grad = 2.0 * coef * dot_split(table, gram)
            for acc in acc_refs:
                grad = grad + acc[at, :]
            new_state = state_ref[at, :] + grad * grad
            new_state_ref[at, :] = new_state
            new_table_ref[at, :] = table - step_size * grad / jnp.sqrt(new_state)
            return carry

        lax.fori_loop(0, rows_dev // step, finish, 0)


def update_rows(row_idx, src_idx, blocks, item_total, table, state, coef, hist_len):
    rows_dev, width = table.shape
    devices = blocks.shape[0]
    sources = 8
    whole = pl.BlockSpec((rows_dev, width), lambda g, r, s: (0, 0))
    return pl.pallas_call(
        functools.partial(update_kernel, sources=sources, coef=coef, hist_len=hist_len),
        grid_spec=pltpu.PrefetchScalarGridSpec(
            num_scalar_prefetch=2,
            grid=(devices // sources,),
            in_specs=[
                pl.BlockSpec((sources, BLOCK_ROWS, width), lambda g, r, s: (g, 0, 0)),
                pl.BlockSpec((width, width), lambda g, r, s: (0, 0)),
                whole,
                whole,
            ],
            out_specs=[whole, whole],
            scratch_shapes=[
                pltpu.VMEM((sources * 2 * LANES, width), f32),
                pltpu.VMEM((width, 2 * width), f32),
            ]
            + [pltpu.VMEM((rows_dev + 8, width), f32)] * CHAINS,
        ),
        out_shape=(
            jax.ShapeDtypeStruct((rows_dev, width), f32),
            jax.ShapeDtypeStruct((rows_dev, width), f32),
        ),
        compiler_params=pltpu.CompilerParams(vmem_limit_bytes=48 * 2**20),
        name="update_rows",
    )(row_idx, src_idx, blocks, item_total, table, state)


def shards(item_table, adagrad_state, history_ids, positive_ids):
    rows_dev, width = item_table.shape
    users_dev, hist_len = history_ids.shape
    devices = lax.axis_size(DP_ROWS)
    coef = penalty_weight / (rows_dev * devices)
    item_gram = jnp.dot(
        item_table.T,
        item_table,
        precision=lax.Precision.HIGHEST,
        preferred_element_type=f32,
    )
    lists = request_lists(history_ids, positive_ids, rows_dev)
    asked = lax.all_to_all(lists, DP_ROWS, split_axis=0, concat_axis=0, tiled=True)
    rows = asked[:, 0, :].astype(i32).reshape(-1)
    codes = asked[:, 1, :]
    place = jnp.arange(devices * LANES, dtype=i32) // LANES % 8 * (2 * LANES)
    src_idx = place + jnp.maximum(codes.astype(i32).reshape(-1), 0)
    here = jnp.stack([lax.axis_index(axis) for axis in DP_ROWS]).astype(i32)
    parts = to_sources(jnp.where(rows < rows_dev, rows, 0), here, item_table, codes, item_gram)
    block = user_block(parts, hist_len)
    blocks = lax.all_gather(block, DP_ROWS)
    item_total = blocks[:, 2 * LANES + 1, :]
    return update_rows(
        rows, src_idx, blocks, item_total, item_table, adagrad_state, coef, hist_len
    )


def solution(mesh):
    finer = Mesh(mesh.devices.reshape(4, 2, 4, 4), DP_ROWS)
    rows = P(DP_ROWS, None)
    return jax.shard_map(
        shards,
        mesh=finer,
        in_specs=(rows, rows, rows, P(DP_ROWS)),
        out_specs=(rows, rows),
        check_vma=False,
    )
```

```python
import functools

import jax
import jax.numpy as jnp
from jax import lax
from jax.experimental import pallas as pl
from jax.experimental.pallas import tpu as pltpu
from jax.sharding import Mesh
from jax.sharding import PartitionSpec as P

X, CORE, Z, Y = "x", "core", "z", "y"
DP_ROWS = (X, CORE, Z, Y)
ORDERS = ((0, 2, 3), (2, 3, 0))

penalty_weight = 10.0
step_size = 0.05

LANES = 128
BLOCK_ROWS = 264
CHAINS = 4

bf16 = jnp.bfloat16
f32 = jnp.float32
i32 = jnp.int32


def iota2(shape, dim):
    return lax.broadcasted_iota(i32, shape, dim)


def split2(x):
    hi = x.astype(bf16)
    lo = (x - hi.astype(f32)).astype(bf16)
    return hi, lo


def dot_f32(a, b):
    return jnp.dot(a, b, preferred_element_type=f32)


def dot_split(a, b):
    ah, al = split2(a)
    bh, bl = split2(b)
    return dot_f32(ah, bh) + (dot_f32(ah, bl) + dot_f32(al, bh))


def half_gram(a):
    hi, lo = split2(a)
    return lax.dot_general(
        hi,
        jnp.concatenate([hi, lo], axis=1),
        (((0,), (0,)), ((), ())),
        preferred_element_type=f32,
    )


def whole_gram(halves):
    cross = halves[:, LANES:]
    return halves[:, :LANES] + (cross + cross.T)


def list_kernel(history_ref, positive_ref, out_ref, *, slots, rows_dev):
    ids_r = jnp.concatenate(
        [history_ref[...], positive_ref[...], jnp.zeros((LANES - slots, LANES), i32)], axis=0
    )
    ids_c = ids_r.T
    sq = (LANES, LANES)
    lane = iota2(sq, 1)
    sub = iota2(sq, 0)
    lane_f = lane.astype(f32)
    one = jnp.ones(sq, f32)
    zero = jnp.zeros(sq, f32)
    lower = jnp.concatenate([jnp.where(sub > lane, one, zero), one], axis=0).astype(bf16)
    ones = one.astype(bf16)
    users = iota2((1, LANES), 1)
    carry = jnp.zeros(sq, f32)
    acc = jnp.zeros((3 * LANES, LANES), f32)
    for h in range(slots):
        owner_c = ids_c[:, h : h + 1] // rows_dev
        member = owner_c == lane
        counts = dot_f32(lower, jnp.where(member, one, zero).astype(bf16))
        mine = jnp.where(member, counts[:LANES] + carry, zero).astype(bf16)
        rank = dot_f32(mine, ones)
        place = jnp.where(rank == lane_f, one, zero).astype(bf16)
        ids = ids_r[h : h + 1, :]
        local = ids % rows_dev
        at_owner = ids // rows_dev == sub
        high = (local // 64 + 1).astype(f32)
        low = (local % 64).astype(f32)
        code = (users + (LANES if h == slots - 1 else 0)).astype(f32)
        vals = jnp.concatenate(
            [
                jnp.where(at_owner, jnp.broadcast_to(high, sq), zero),
                jnp.where(at_owner, jnp.broadcast_to(low, sq), zero),
                jnp.where(at_owner, jnp.broadcast_to(code, sq), zero),
            ],
            axis=0,
        ).astype(bf16)
        acc = acc + dot_f32(vals, place)
        carry = carry + counts[LANES:]
    high = acc[:LANES].astype(i32)
    low = acc[LANES : 2 * LANES].astype(i32)
    code = acc[2 * LANES :].astype(i32)
    present = high > 0
    code = jnp.where(present, code, -1)
    out_ref[:, 0, :] = jnp.where(present, (high - 1) * 64 + low, rows_dev).astype(f32)
    out_ref[:, 1, :] = code.astype(f32)


def request_lists(history_ids, positive_ids, rows_dev):
    users, hist_len = history_ids.shape
    return pl.pallas_call(
        functools.partial(list_kernel, slots=hist_len + 1, rows_dev=rows_dev),
        out_shape=jax.ShapeDtypeStruct((LANES, 2, LANES), f32),
        name="request_lists",
    )(history_ids.T, positive_ids.reshape(1, users))


def partial_kernel(rows_ref, plane_ref, table_ref, codes_ref, gram_ref, *refs, first, first_step):
    from_ref = refs[0] if len(refs) == 10 else None
    out_ref = refs[-9]
    picked_refs = refs[-8:]
    code_of = iota2((2 * LANES, LANES), 0).astype(f32)
    one = jnp.ones((2 * LANES, LANES), f32)
    zero = jnp.zeros((2 * LANES, LANES), f32)
    unroll = 32
    offsets = (first + first_step * pl.program_id(0), 2 * pl.program_id(1))
    at_first = ((plane_ref[1] + offsets[0]) & 3) * plane_ref[4]
    for k in range(2):
        at_second = ((plane_ref[2] + (offsets[1] + k)) & 3) * plane_ref[5]
        for j in range(4):
            at_third = ((plane_ref[3] + j) & 3) * plane_ref[6]
            source = plane_ref[0] + at_first + at_second + at_third
            base = source * LANES
            picked_ref = picked_refs[4 * k + j]
            for at in range(0, LANES, unroll):
                picked = [
                    table_ref[pl.ds(rows_ref[base + (at + i)], 1), :] for i in range(unroll)
                ]
                for i in range(unroll):
                    picked_ref[at + i : at + i + 1, :] = picked[i]
            weight = jnp.where(codes_ref[pl.ds(source, 1), :] == code_of, one, zero)
            weight = weight.astype(bf16)
            block = dot_f32(
                jnp.concatenate([weight, weight], axis=1),
                jnp.concatenate(split2(picked_ref[...]), axis=0),
            )
            gram = jnp.broadcast_to(gram_ref[pl.ds(source, 1), :], (8, LANES))
            if from_ref is not None:
                block = block + from_ref[0, k, j, : 2 * LANES, :]
                gram = gram + from_ref[0, k, j, 2 * LANES :, :]
            out_ref[0, k, j, : 2 * LANES, :] = block
            out_ref[0, k, j, 2 * LANES :, :] = gram


def partial_sums(rows_idx, plane, table, codes, gram, firsts, received=None, place=0):
    rows_dev, width = table.shape
    n = len(firsts)
    block = (1, 2, 4, BLOCK_ROWS, width)

    def whole(shape):
        return pl.BlockSpec(shape, lambda i, k, r, p: (0,) * len(shape))

    in_specs = [whole((rows_dev, width)), whole(codes.shape), whole(gram.shape)]
    operands = (rows_idx, plane, table, codes, gram)
    if received is not None:
        in_specs.append(pl.BlockSpec(block, lambda i, k, r, p: (place, k, 0, 0, 0)))
        operands += (received,)
    return pl.pallas_call(
        functools.partial(
            partial_kernel, first=firsts[0], first_step=firsts[-1] - firsts[0]
        ),
        grid_spec=pltpu.PrefetchScalarGridSpec(
            num_scalar_prefetch=2,
            grid=(n, 2),
            in_specs=in_specs,
            out_specs=pl.BlockSpec(block, lambda i, k, r, p: (i, k, 0, 0, 0)),
            scratch_shapes=[pltpu.VMEM((LANES, width), f32)] * 8,
        ),
        out_shape=jax.ShapeDtypeStruct((n, 4, 4, BLOCK_ROWS, width), f32),
        compiler_params=pltpu.CompilerParams(vmem_limit_bytes=32 * 2**20),
        name="partial_sums",
    )(*operands)


def split_sum_kernel(*refs):
    pieces, outs = refs[:4], refs[4:]
    for i in range(4):
        outs[i][...] = (pieces[0][i] + pieces[1][i]) + (pieces[2][i] + pieces[3][i])


def split_sums(pieces, name):
    return pl.pallas_call(
        split_sum_kernel,
        out_shape=[jax.ShapeDtypeStruct(pieces[0].shape[1:], f32)] * 4,
        compiler_params=pltpu.CompilerParams(vmem_limit_bytes=40 * 2**20),
        name=name,
    )(*pieces)


def along(stage, by):
    pairs = []
    for device in range(128):
        at = [device // 32, device // 16 % 2, device // 4 % 4, device % 4]
        axis = ORDERS[at[1]][stage]
        at[axis] = (at[axis] + by) % 4
        pairs.append((device, ((at[0] * 2 + at[1]) * 4 + at[2]) * 4 + at[3]))
    return pairs


def shifted(array, stage, by):
    return lax.ppermute(array, DP_ROWS, along(stage, by)) if by else array


def plane_of(core):
    here = jnp.stack([lax.axis_index(axis) for axis in DP_ROWS]).astype(i32)
    strides = jnp.array([32, 16, 4, 1], i32)
    orders = [jnp.array(order, i32) for order in ORDERS]
    order = jnp.where(core == 0, orders[0], orders[1])
    chosen = order[:, None] == jnp.arange(4, dtype=i32)[None, :]
    at = jnp.sum(jnp.where(chosen, here[None, :], 0), axis=1)
    stride = jnp.sum(jnp.where(chosen, strides[None, :], 0), axis=1)
    return jnp.concatenate([(core * 16)[None], at, stride])


def to_sources(rows_idx, table, codes, gram):
    core = lax.axis_index(CORE).astype(i32)
    other, own = plane_of(1 - core), plane_of(core)
    swap = [(0, 1), (1, 0)]
    received = []
    for firsts in ((1, 3), (2, 0)):
        mine = partial_sums(rows_idx, other, table, codes, gram, firsts)
        received.append(lax.ppermute(mine, CORE, swap))
    pieces = [None] * 4
    for k, first in enumerate((1, 3, 2, 0)):
        block = partial_sums(
            rows_idx, own, table, codes, gram, (first,), received[k // 2], k % 2
        )
        pieces[first] = shifted(block.reshape(block.shape[1:]), 0, first)
    for stage in (1, 2):
        parts = split_sums(pieces, f"sum_stage_{stage}")
        pieces = [shifted(part, stage, by) for by, part in enumerate(parts)]
    return pieces


def user_kernel(*refs, hist_len):
    out_ref = refs[4]
    sums = (refs[0][...] + refs[1][...]) + (refs[2][...] + refs[3][...])
    user = sums[:LANES] / hist_len
    positive = sums[LANES : 2 * LANES]
    gap = jnp.sum(user * positive, axis=1, keepdims=True) - 1.0
    sq = (LANES, LANES)
    gap_row = jnp.sum(
        jnp.where(iota2(sq, 0) == iota2(sq, 1), jnp.broadcast_to(gap, sq), 0.0),
        axis=0,
        keepdims=True,
    )
    out_ref[:LANES, :] = positive
    out_ref[LANES : 2 * LANES, :] = user
    tail = (8, LANES)
    out_ref[2 * LANES :, :] = jnp.where(
        iota2(tail, 0) == 0,
        jnp.broadcast_to(gap_row, tail),
        sums[2 * LANES :],
    )


def user_block(pieces, hist_len):
    return pl.pallas_call(
        functools.partial(user_kernel, hist_len=hist_len),
        out_shape=jax.ShapeDtypeStruct(pieces[0].shape, f32),
        name="user_block",
    )(*pieces)


def update_kernel(
    row_idx_ref, src_idx_ref, blocks_ref, item_ref, table_ref, state_ref, new_table_ref, new_state_ref,
    stage_ref, gram_ref, *acc_refs, sources, coef, hist_len,
):
    g = pl.program_id(0)
    rows_dev = table_ref.shape[0]
    sq = (LANES, LANES)

    @pl.when(g == 0)
    def _():
        gram_ref[...] = jnp.zeros_like(gram_ref)
        for acc in acc_refs:
            acc[...] = jnp.zeros_like(acc)

    diagonal = iota2(sq, 0) == iota2(sq, 1)
    users = jnp.concatenate(
        [blocks_ref[s, LANES : 2 * LANES, :] for s in range(sources)], axis=0
    )
    pulls = dot_split(users, item_ref[...])
    for s in range(sources):
        user = blocks_ref[s, LANES : 2 * LANES, :]
        gap_row = blocks_ref[s, 2 * LANES : 2 * LANES + 1, :]
        gap = 2.0 * jnp.sum(
            jnp.where(diagonal, jnp.broadcast_to(gap_row, sq), 0.0), axis=1, keepdims=True
        )
        pull = pulls[LANES * s : LANES * (s + 1)]
        grad = gap * blocks_ref[s, :LANES, :] + 2.0 * coef * pull
        stage_ref[2 * LANES * s : 2 * LANES * s + LANES, :] = grad / hist_len
        stage_ref[2 * LANES * s + LANES : 2 * LANES * (s + 1), :] = gap * user
    gram_ref[...] += half_gram(users)

    base = g * (sources * LANES)
    unroll = 128

    def body(j, carry):
        for at in range(0, unroll, CHAINS):
            first = base + j * unroll + at
            rows = [row_idx_ref[first + k] for k in range(CHAINS)]
            srcs = [src_idx_ref[first + k] for k in range(CHAINS)]
            grads = [stage_ref[pl.ds(srcs[k], 1), :] for k in range(CHAINS)]
            sums = [acc_refs[k][pl.ds(rows[k], 1), :] + grads[k] for k in range(CHAINS)]
            for k in range(CHAINS):
                acc_refs[k][pl.ds(rows[k], 1), :] = sums[k]
        return carry

    lax.fori_loop(0, sources * LANES // unroll, body, 0)

    @pl.when(g == pl.num_programs(0) - 1)
    def _():
        step = 512
        gram = whole_gram(gram_ref[...])

        def finish(i, carry):
            at = pl.ds(pl.multiple_of(i * step, step), step)
            table = table_ref[at, :]
            grad = 2.0 * coef * dot_split(table, gram)
            for acc in acc_refs:
                grad = grad + acc[at, :]
            new_state = state_ref[at, :] + grad * grad
            new_state_ref[at, :] = new_state
            new_table_ref[at, :] = table - step_size * grad / jnp.sqrt(new_state)
            return carry

        lax.fori_loop(0, rows_dev // step, finish, 0)


def update_rows(row_idx, src_idx, blocks, item_total, table, state, coef, hist_len):
    rows_dev, width = table.shape
    devices = blocks.shape[0]
    sources = 16
    whole = pl.BlockSpec((rows_dev, width), lambda g, r, s: (0, 0))
    return pl.pallas_call(
        functools.partial(update_kernel, sources=sources, coef=coef, hist_len=hist_len),
        grid_spec=pltpu.PrefetchScalarGridSpec(
            num_scalar_prefetch=2,
            grid=(devices // sources,),
            in_specs=[
                pl.BlockSpec((sources, BLOCK_ROWS, width), lambda g, r, s: (g, 0, 0)),
                pl.BlockSpec((width, width), lambda g, r, s: (0, 0)),
                whole,
                whole,
            ],
            out_specs=[whole, whole],
            scratch_shapes=[
                pltpu.VMEM((sources * 2 * LANES, width), f32),
                pltpu.VMEM((width, 2 * width), f32),
            ]
            + [pltpu.VMEM((rows_dev + 8, width), f32)] * CHAINS,
        ),
        out_shape=(
            jax.ShapeDtypeStruct((rows_dev, width), f32),
            jax.ShapeDtypeStruct((rows_dev, width), f32),
        ),
        compiler_params=pltpu.CompilerParams(vmem_limit_bytes=48 * 2**20),
        name="update_rows",
    )(row_idx, src_idx, blocks, item_total, table, state)


def shards(item_table, adagrad_state, history_ids, positive_ids):
    rows_dev, width = item_table.shape
    users_dev, hist_len = history_ids.shape
    devices = lax.axis_size(DP_ROWS)
    coef = penalty_weight / (rows_dev * devices)
    item_gram = jnp.dot(
        item_table.T,
        item_table,
        precision=lax.Precision.HIGHEST,
        preferred_element_type=f32,
    )
    lists = request_lists(history_ids, positive_ids, rows_dev)
    asked = lax.all_to_all(lists, DP_ROWS, split_axis=0, concat_axis=0, tiled=True)
    rows = asked[:, 0, :].astype(i32).reshape(-1)
    codes = asked[:, 1, :]
    place = jnp.arange(devices * LANES, dtype=i32) // LANES % 16 * (2 * LANES)
    src_idx = place + jnp.maximum(codes.astype(i32).reshape(-1), 0)
    pieces = to_sources(jnp.where(rows < rows_dev, rows, 0), item_table, codes, item_gram)
    block = user_block(pieces, hist_len)
    blocks = lax.all_gather(block, DP_ROWS)
    item_total = blocks[:, 2 * LANES + 1, :]
    return update_rows(
        rows, src_idx, blocks, item_total, item_table, adagrad_state, coef, hist_len
    )


def solution(mesh):
    finer = Mesh(mesh.devices.reshape(4, 2, 4, 4), DP_ROWS)
    rows = P(DP_ROWS, None)
    return jax.shard_map(
        shards,
        mesh=finer,
        in_specs=(rows, rows, rows, P(DP_ROWS)),
        out_specs=(rows, rows),
        check_vma=False,
    )
```

```python
import functools

import jax
import jax.numpy as jnp
from jax import lax
from jax.experimental import pallas as pl
from jax.experimental.pallas import tpu as pltpu
from jax.sharding import Mesh
from jax.sharding import PartitionSpec as P

X, CORE, Z, Y = "x", "core", "z", "y"
DP_ROWS = (X, CORE, Z, Y)
ORDERS = ((0, 2, 3), (2, 3, 0))

penalty_weight = 10.0
step_size = 0.05

LANES = 128
BLOCK_ROWS = 264
GROUP = 4
CHAINS = 4

bf16 = jnp.bfloat16
f32 = jnp.float32
i32 = jnp.int32


def iota2(shape, dim):
    return lax.broadcasted_iota(i32, shape, dim)


def split2(x):
    hi = x.astype(bf16)
    lo = (x - hi.astype(f32)).astype(bf16)
    return hi, lo


def dot_f32(a, b):
    return jnp.dot(a, b, preferred_element_type=f32)


def dot_split(a, b):
    ah, al = split2(a)
    bh, bl = split2(b)
    return dot_f32(ah, bh) + (dot_f32(ah, bl) + dot_f32(al, bh))


def half_gram(a):
    hi, lo = split2(a)
    return lax.dot_general(
        hi,
        jnp.concatenate([hi, lo], axis=1),
        (((0,), (0,)), ((), ())),
        preferred_element_type=f32,
    )


def whole_gram(halves):
    cross = halves[:, LANES:]
    return halves[:, :LANES] + (cross + cross.T)


def list_kernel(history_ref, positive_ref, out_ref, *, slots, rows_dev):
    shift = rows_dev.bit_length() - 1
    sq = (LANES, LANES)
    ids = jnp.concatenate(
        [history_ref[...], positive_ref[...], jnp.full((LANES - slots, LANES), -1, i32)], axis=0
    )
    owner_r = lax.shift_right_arithmetic(ids, shift)
    owner_c = owner_r.T
    local = ids & (rows_dev - 1)
    high_r = (lax.shift_right_logical(local, 6) + 1).astype(f32)
    low_r = (local & 63).astype(f32)
    users = iota2((1, LANES), 1).astype(f32)
    lane = iota2(sq, 1)
    sub = iota2(sq, 0)
    lane_f = lane.astype(f32)
    one = jnp.ones(sq, f32)
    zero = jnp.zeros(sq, f32)
    lower = jnp.concatenate([jnp.where(sub > lane, one, zero), one], axis=0).astype(bf16)
    ones = one.astype(bf16)
    carry = jnp.zeros(sq, f32)
    acc = jnp.zeros((3 * LANES, LANES), f32)
    for start in range(0, slots, GROUP):
        group = range(start, start + GROUP)
        members = [owner_c[:, h : h + 1] == lane for h in group]
        counts = dot_f32(
            lower,
            jnp.concatenate([jnp.where(m, one, zero) for m in members], axis=1).astype(bf16),
        )
        mine = []
        for k, member in enumerate(members):
            block = counts[:, k * LANES : (k + 1) * LANES]
            mine.append(jnp.where(member, block[:LANES] + carry, zero))
            carry = carry + block[LANES:]
        rank = dot_f32(jnp.concatenate(mine, axis=0).astype(bf16), ones)
        place = jnp.where(rank == jnp.concatenate([lane_f] * GROUP, axis=0), 1.0, 0.0)
        vals = []
        for h in group:
            at_owner = owner_r[h : h + 1, :] == sub
            code = users + (LANES if h == slots - 1 else 0)
            vals.append(
                jnp.concatenate(
                    [
                        jnp.where(at_owner, jnp.broadcast_to(value, sq), zero)
                        for value in (high_r[h : h + 1, :], low_r[h : h + 1, :], code)
                    ],
                    axis=0,
                )
            )
        acc = acc + dot_f32(jnp.concatenate(vals, axis=1).astype(bf16), place.astype(bf16))
    high = acc[:LANES].astype(i32)
    low = acc[LANES : 2 * LANES].astype(i32)
    code = acc[2 * LANES :].astype(i32)
    present = high > 0
    out_ref[:, 0, :] = jnp.where(present, (high - 1) * 64 + low, rows_dev).astype(f32)
    out_ref[:, 1, :] = jnp.where(present, code, -1).astype(f32)


def request_lists(history_ids, positive_ids, rows_dev):
    users, hist_len = history_ids.shape
    return pl.pallas_call(
        functools.partial(list_kernel, slots=hist_len + 1, rows_dev=rows_dev),
        out_shape=jax.ShapeDtypeStruct((LANES, 2, LANES), f32),
        name="request_lists",
    )(history_ids.T, positive_ids.reshape(1, users))


def partial_kernel(rows_ref, plane_ref, table_ref, codes_ref, gram_ref, *refs, first, first_step):
    from_ref = refs[0] if len(refs) == 10 else None
    out_ref = refs[-9]
    picked_refs = refs[-8:]
    code_of = iota2((2 * LANES, LANES), 0).astype(f32)
    one = jnp.ones((2 * LANES, LANES), f32)
    zero = jnp.zeros((2 * LANES, LANES), f32)
    unroll = 32
    offsets = (first + first_step * pl.program_id(0), 2 * pl.program_id(1))
    at_first = ((plane_ref[1] + offsets[0]) & 3) * plane_ref[4]
    for k in range(2):
        at_second = ((plane_ref[2] + (offsets[1] + k)) & 3) * plane_ref[5]
        for j in range(4):
            at_third = ((plane_ref[3] + j) & 3) * plane_ref[6]
            source = plane_ref[0] + at_first + at_second + at_third
            base = source * LANES
            picked_ref = picked_refs[4 * k + j]
            for at in range(0, LANES, unroll):
                picked = [
                    table_ref[pl.ds(rows_ref[base + (at + i)], 1), :] for i in range(unroll)
                ]
                for i in range(unroll):
                    picked_ref[at + i : at + i + 1, :] = picked[i]
            weight = jnp.where(codes_ref[pl.ds(source, 1), :] == code_of, one, zero)
            weight = weight.astype(bf16)
            block = dot_f32(
                jnp.concatenate([weight, weight], axis=1),
                jnp.concatenate(split2(picked_ref[...]), axis=0),
            )
            gram = jnp.broadcast_to(gram_ref[pl.ds(source, 1), :], (8, LANES))
            if from_ref is not None:
                block = block + from_ref[0, k, j, : 2 * LANES, :]
                gram = gram + from_ref[0, k, j, 2 * LANES :, :]
            out_ref[0, k, j, : 2 * LANES, :] = block
            out_ref[0, k, j, 2 * LANES :, :] = gram


def partial_sums(rows_idx, plane, table, codes, gram, firsts, received=None, place=0):
    rows_dev, width = table.shape
    n = len(firsts)
    block = (1, 2, 4, BLOCK_ROWS, width)

    def whole(shape):
        return pl.BlockSpec(shape, lambda i, k, r, p: (0,) * len(shape))

    in_specs = [whole((rows_dev, width)), whole(codes.shape), whole(gram.shape)]
    operands = (rows_idx, plane, table, codes, gram)
    if received is not None:
        in_specs.append(pl.BlockSpec(block, lambda i, k, r, p: (place, k, 0, 0, 0)))
        operands += (received,)
    return pl.pallas_call(
        functools.partial(
            partial_kernel, first=firsts[0], first_step=firsts[-1] - firsts[0]
        ),
        grid_spec=pltpu.PrefetchScalarGridSpec(
            num_scalar_prefetch=2,
            grid=(n, 2),
            in_specs=in_specs,
            out_specs=pl.BlockSpec(block, lambda i, k, r, p: (i, k, 0, 0, 0)),
            scratch_shapes=[pltpu.VMEM((LANES, width), f32)] * 8,
        ),
        out_shape=jax.ShapeDtypeStruct((n, 4, 4, BLOCK_ROWS, width), f32),
        compiler_params=pltpu.CompilerParams(vmem_limit_bytes=32 * 2**20),
        name="partial_sums",
    )(*operands)


def split_sum_kernel(*refs):
    pieces, outs = refs[:4], refs[4:]
    for i in range(4):
        outs[i][...] = (pieces[0][i] + pieces[1][i]) + (pieces[2][i] + pieces[3][i])


def split_sums(pieces, name):
    return pl.pallas_call(
        split_sum_kernel,
        out_shape=[jax.ShapeDtypeStruct(pieces[0].shape[1:], f32)] * 4,
        compiler_params=pltpu.CompilerParams(vmem_limit_bytes=40 * 2**20),
        name=name,
    )(*pieces)


def along(stage, by):
    pairs = []
    for device in range(128):
        at = [device // 32, device // 16 % 2, device // 4 % 4, device % 4]
        axis = ORDERS[at[1]][stage]
        at[axis] = (at[axis] + by) % 4
        pairs.append((device, ((at[0] * 2 + at[1]) * 4 + at[2]) * 4 + at[3]))
    return pairs


def shifted(array, stage, by):
    return lax.ppermute(array, DP_ROWS, along(stage, by)) if by else array


def plane_of(core):
    here = jnp.stack([lax.axis_index(axis) for axis in DP_ROWS]).astype(i32)
    strides = jnp.array([32, 16, 4, 1], i32)
    orders = [jnp.array(order, i32) for order in ORDERS]
    order = jnp.where(core == 0, orders[0], orders[1])
    chosen = order[:, None] == jnp.arange(4, dtype=i32)[None, :]
    at = jnp.sum(jnp.where(chosen, here[None, :], 0), axis=1)
    stride = jnp.sum(jnp.where(chosen, strides[None, :], 0), axis=1)
    return jnp.concatenate([(core * 16)[None], at, stride])


def to_sources(rows_idx, table, codes, gram):
    core = lax.axis_index(CORE).astype(i32)
    other, own = plane_of(1 - core), plane_of(core)
    swap = [(0, 1), (1, 0)]
    received = []
    for firsts in ((1, 3), (2, 0)):
        mine = partial_sums(rows_idx, other, table, codes, gram, firsts)
        received.append(lax.ppermute(mine, CORE, swap))
    pieces = [None] * 4
    for k, first in enumerate((1, 3, 2, 0)):
        block = partial_sums(
            rows_idx, own, table, codes, gram, (first,), received[k // 2], k % 2
        )
        pieces[first] = shifted(block.reshape(block.shape[1:]), 0, first)
    for stage in (1, 2):
        parts = split_sums(pieces, f"sum_stage_{stage}")
        pieces = [shifted(part, stage, by) for by, part in enumerate(parts)]
    return pieces


def user_kernel(*refs, hist_len):
    out_ref = refs[4]
    sums = (refs[0][...] + refs[1][...]) + (refs[2][...] + refs[3][...])
    user = sums[:LANES] / hist_len
    positive = sums[LANES : 2 * LANES]
    gap = jnp.sum(user * positive, axis=1, keepdims=True) - 1.0
    sq = (LANES, LANES)
    gap_row = jnp.sum(
        jnp.where(iota2(sq, 0) == iota2(sq, 1), jnp.broadcast_to(gap, sq), 0.0),
        axis=0,
        keepdims=True,
    )
    out_ref[:LANES, :] = positive
    out_ref[LANES : 2 * LANES, :] = user
    tail = (8, LANES)
    out_ref[2 * LANES :, :] = jnp.where(
        iota2(tail, 0) == 0,
        jnp.broadcast_to(gap_row, tail),
        sums[2 * LANES :],
    )


def user_block(pieces, hist_len):
    return pl.pallas_call(
        functools.partial(user_kernel, hist_len=hist_len),
        out_shape=jax.ShapeDtypeStruct(pieces[0].shape, f32),
        name="user_block",
    )(*pieces)


def update_kernel(
    row_idx_ref, src_idx_ref, blocks_ref, item_ref, table_ref, state_ref, new_table_ref, new_state_ref,
    stage_ref, gram_ref, *acc_refs, sources, coef, hist_len,
):
    g = pl.program_id(0)
    rows_dev = table_ref.shape[0]
    sq = (LANES, LANES)

    @pl.when(g == 0)
    def _():
        gram_ref[...] = jnp.zeros_like(gram_ref)
        for acc in acc_refs:
            acc[...] = jnp.zeros_like(acc)

    diagonal = iota2(sq, 0) == iota2(sq, 1)
    users = jnp.concatenate(
        [blocks_ref[s, LANES : 2 * LANES, :] for s in range(sources)], axis=0
    )
    pulls = dot_split(users, item_ref[...])
    for s in range(sources):
        user = blocks_ref[s, LANES : 2 * LANES, :]
        gap_row = blocks_ref[s, 2 * LANES : 2 * LANES + 1, :]
        gap = 2.0 * jnp.sum(
            jnp.where(diagonal, jnp.broadcast_to(gap_row, sq), 0.0), axis=1, keepdims=True
        )
        pull = pulls[LANES * s : LANES * (s + 1)]
        grad = gap * blocks_ref[s, :LANES, :] + 2.0 * coef * pull
        stage_ref[2 * LANES * s : 2 * LANES * s + LANES, :] = grad / hist_len
        stage_ref[2 * LANES * s + LANES : 2 * LANES * (s + 1), :] = gap * user
    gram_ref[...] += half_gram(users)

    base = g * (sources * LANES)
    unroll = 128

    def body(j, carry):
        for at in range(0, unroll, CHAINS):
            first = base + j * unroll + at
            rows = [row_idx_ref[first + k] for k in range(CHAINS)]
            srcs = [src_idx_ref[first + k] for k in range(CHAINS)]
            grads = [stage_ref[pl.ds(srcs[k], 1), :] for k in range(CHAINS)]
            sums = [acc_refs[k][pl.ds(rows[k], 1), :] + grads[k] for k in range(CHAINS)]
            for k in range(CHAINS):
                acc_refs[k][pl.ds(rows[k], 1), :] = sums[k]
        return carry

    lax.fori_loop(0, sources * LANES // unroll, body, 0)

    @pl.when(g == pl.num_programs(0) - 1)
    def _():
        step = 512
        gram = whole_gram(gram_ref[...])

        def finish(i, carry):
            at = pl.ds(pl.multiple_of(i * step, step), step)
            table = table_ref[at, :]
            grad = 2.0 * coef * dot_split(table, gram)
            for acc in acc_refs:
                grad = grad + acc[at, :]
            new_state = state_ref[at, :] + grad * grad
            new_state_ref[at, :] = new_state
            new_table_ref[at, :] = table - step_size * grad / jnp.sqrt(new_state)
            return carry

        lax.fori_loop(0, rows_dev // step, finish, 0)


def update_rows(row_idx, src_idx, blocks, item_total, table, state, coef, hist_len):
    rows_dev, width = table.shape
    devices = blocks.shape[0]
    sources = 16
    whole = pl.BlockSpec((rows_dev, width), lambda g, r, s: (0, 0))
    return pl.pallas_call(
        functools.partial(update_kernel, sources=sources, coef=coef, hist_len=hist_len),
        grid_spec=pltpu.PrefetchScalarGridSpec(
            num_scalar_prefetch=2,
            grid=(devices // sources,),
            in_specs=[
                pl.BlockSpec((sources, BLOCK_ROWS, width), lambda g, r, s: (g, 0, 0)),
                pl.BlockSpec((width, width), lambda g, r, s: (0, 0)),
                whole,
                whole,
            ],
            out_specs=[whole, whole],
            scratch_shapes=[
                pltpu.VMEM((sources * 2 * LANES, width), f32),
                pltpu.VMEM((width, 2 * width), f32),
            ]
            + [pltpu.VMEM((rows_dev + 8, width), f32)] * CHAINS,
        ),
        out_shape=(
            jax.ShapeDtypeStruct((rows_dev, width), f32),
            jax.ShapeDtypeStruct((rows_dev, width), f32),
        ),
        compiler_params=pltpu.CompilerParams(vmem_limit_bytes=48 * 2**20),
        name="update_rows",
    )(row_idx, src_idx, blocks, item_total, table, state)


def shards(item_table, adagrad_state, history_ids, positive_ids):
    rows_dev, width = item_table.shape
    users_dev, hist_len = history_ids.shape
    devices = lax.axis_size(DP_ROWS)
    coef = penalty_weight / (rows_dev * devices)
    item_gram = jnp.dot(
        item_table.T,
        item_table,
        precision=lax.Precision.HIGHEST,
        preferred_element_type=f32,
    )
    lists = request_lists(history_ids, positive_ids, rows_dev)
    asked = lax.all_to_all(lists, DP_ROWS, split_axis=0, concat_axis=0, tiled=True)
    rows = asked[:, 0, :].astype(i32).reshape(-1)
    codes = asked[:, 1, :]
    place = jnp.arange(devices * LANES, dtype=i32) // LANES % 16 * (2 * LANES)
    src_idx = place + jnp.maximum(codes.astype(i32).reshape(-1), 0)
    pieces = to_sources(jnp.where(rows < rows_dev, rows, 0), item_table, codes, item_gram)
    block = user_block(pieces, hist_len)
    blocks = lax.all_gather(block, DP_ROWS)
    item_total = blocks[:, 2 * LANES + 1, :]
    return update_rows(
        rows, src_idx, blocks, item_total, item_table, adagrad_state, coef, hist_len
    )


def solution(mesh):
    finer = Mesh(mesh.devices.reshape(4, 2, 4, 4), DP_ROWS)
    rows = P(DP_ROWS, None)
    return jax.shard_map(
        shards,
        mesh=finer,
        in_specs=(rows, rows, rows, P(DP_ROWS)),
        out_specs=(rows, rows),
        check_vma=False,
    )
```

```python
import functools

import jax
import jax.numpy as jnp
from jax import lax
from jax.experimental import pallas as pl
from jax.experimental.pallas import tpu as pltpu
from jax.sharding import Mesh
from jax.sharding import PartitionSpec as P

X, CORE, Z, Y = "x", "core", "z", "y"
DP_ROWS = (X, CORE, Z, Y)
ORDERS = ((0, 2, 3), (2, 3, 0))

penalty_weight = 10.0
step_size = 0.05

LANES = 128
SUM_ROWS = 256
BLOCK_ROWS = 264
TOTAL_COPIES = 16
GROUP = 4
CHAINS = 4

bf16 = jnp.bfloat16
f32 = jnp.float32
i32 = jnp.int32


def iota2(shape, dim):
    return lax.broadcasted_iota(i32, shape, dim)


def split2(x):
    hi = x.astype(bf16)
    lo = (x - hi.astype(f32)).astype(bf16)
    return hi, lo


def dot_f32(a, b):
    return jnp.dot(a, b, preferred_element_type=f32)


def dot_split(a, b):
    ah, al = split2(a)
    bh, bl = split2(b)
    return dot_f32(ah, bh) + (dot_f32(ah, bl) + dot_f32(al, bh))


def half_gram(a):
    hi, lo = split2(a)
    return lax.dot_general(
        hi,
        jnp.concatenate([hi, lo], axis=1),
        (((0,), (0,)), ((), ())),
        preferred_element_type=f32,
    )


def whole_gram(halves):
    cross = halves[:, LANES:]
    return halves[:, :LANES] + (cross + cross.T)


def list_kernel(history_ref, positive_ref, gram_ref, out_ref, *, slots, rows_dev):
    shift = rows_dev.bit_length() - 1
    sq = (LANES, LANES)
    ids = jnp.concatenate(
        [history_ref[...], positive_ref[...], jnp.full((LANES - slots, LANES), -1, i32)], axis=0
    )
    owner_r = lax.shift_right_arithmetic(ids, shift)
    owner_c = owner_r.T
    local = ids & (rows_dev - 1)
    high_r = (lax.shift_right_logical(local, 6) + 1).astype(f32)
    low_r = (local & 63).astype(f32)
    users = iota2((1, LANES), 1).astype(f32)
    lane = iota2(sq, 1)
    sub = iota2(sq, 0)
    lane_f = lane.astype(f32)
    one = jnp.ones(sq, f32)
    zero = jnp.zeros(sq, f32)
    lower = jnp.concatenate([jnp.where(sub > lane, one, zero), one], axis=0).astype(bf16)
    ones = one.astype(bf16)
    carry = jnp.zeros(sq, f32)
    acc = jnp.zeros((3 * LANES, LANES), f32)
    for start in range(0, slots, GROUP):
        group = range(start, start + GROUP)
        members = [owner_c[:, h : h + 1] == lane for h in group]
        counts = dot_f32(
            lower,
            jnp.concatenate([jnp.where(m, one, zero) for m in members], axis=1).astype(bf16),
        )
        mine = []
        for k, member in enumerate(members):
            block = counts[:, k * LANES : (k + 1) * LANES]
            mine.append(jnp.where(member, block[:LANES] + carry, zero))
            carry = carry + block[LANES:]
        rank = dot_f32(jnp.concatenate(mine, axis=0).astype(bf16), ones)
        place = jnp.where(rank == jnp.concatenate([lane_f] * GROUP, axis=0), 1.0, 0.0)
        vals = []
        for h in group:
            at_owner = owner_r[h : h + 1, :] == sub
            code = users + (LANES if h == slots - 1 else 0)
            vals.append(
                jnp.concatenate(
                    [
                        jnp.where(at_owner, jnp.broadcast_to(value, sq), zero)
                        for value in (high_r[h : h + 1, :], low_r[h : h + 1, :], code)
                    ],
                    axis=0,
                )
            )
        acc = acc + dot_f32(jnp.concatenate(vals, axis=1).astype(bf16), place.astype(bf16))
    high = acc[:LANES].astype(i32)
    low = acc[LANES : 2 * LANES].astype(i32)
    code = acc[2 * LANES :].astype(i32)
    present = high > 0
    out_ref[:, 0, :] = jnp.where(present, (high - 1) * 64 + low, rows_dev).astype(f32)
    out_ref[:, 1, :] = jnp.where(present, code, -1).astype(f32)
    out_ref[:, 2, :] = gram_ref[...]
    out_ref[:, 3, :] = zero


def request_lists(history_ids, positive_ids, gram, rows_dev):
    users, hist_len = history_ids.shape
    return pl.pallas_call(
        functools.partial(list_kernel, slots=hist_len + 1, rows_dev=rows_dev),
        out_shape=jax.ShapeDtypeStruct((LANES, 4, LANES), f32),
        name="request_lists",
    )(history_ids.T, positive_ids.reshape(1, users), gram)


def partial_kernel(rows_ref, plane_ref, table_ref, codes_ref, *refs, first, first_step):
    from_ref = refs[0] if len(refs) == 10 else None
    out_ref = refs[-9]
    picked_refs = refs[-8:]
    code_of = iota2((2 * LANES, LANES), 0).astype(f32)
    one = jnp.ones((2 * LANES, LANES), f32)
    zero = jnp.zeros((2 * LANES, LANES), f32)
    unroll = 32
    offsets = (first + first_step * pl.program_id(0), 2 * pl.program_id(1))
    at_first = ((plane_ref[1] + offsets[0]) & 3) * plane_ref[4]
    for k in range(2):
        at_second = ((plane_ref[2] + (offsets[1] + k)) & 3) * plane_ref[5]
        for j in range(4):
            at_third = ((plane_ref[3] + j) & 3) * plane_ref[6]
            source = plane_ref[0] + at_first + at_second + at_third
            base = source * LANES
            picked_ref = picked_refs[4 * k + j]
            for at in range(0, LANES, unroll):
                picked = [
                    table_ref[pl.ds(rows_ref[base + (at + i)], 1), :] for i in range(unroll)
                ]
                for i in range(unroll):
                    picked_ref[at + i : at + i + 1, :] = picked[i]
            weight = jnp.where(codes_ref[pl.ds(source, 1), :] == code_of, one, zero)
            weight = weight.astype(bf16)
            block = dot_f32(
                jnp.concatenate([weight, weight], axis=1),
                jnp.concatenate(split2(picked_ref[...]), axis=0),
            )
            if from_ref is not None:
                block = block + from_ref[0, k, j]
            out_ref[0, k, j] = block


def partial_sums(rows_idx, plane, table, codes, firsts, received=None, place=0):
    rows_dev, width = table.shape
    n = len(firsts)
    block = (1, 2, 4, SUM_ROWS, width)

    def whole(shape):
        return pl.BlockSpec(shape, lambda i, k, r, p: (0,) * len(shape))

    in_specs = [whole((rows_dev, width)), whole(codes.shape)]
    operands = (rows_idx, plane, table, codes)
    if received is not None:
        in_specs.append(pl.BlockSpec(block, lambda i, k, r, p: (place, k, 0, 0, 0)))
        operands += (received,)
    return pl.pallas_call(
        functools.partial(
            partial_kernel, first=firsts[0], first_step=firsts[-1] - firsts[0]
        ),
        grid_spec=pltpu.PrefetchScalarGridSpec(
            num_scalar_prefetch=2,
            grid=(n, 2),
            in_specs=in_specs,
            out_specs=pl.BlockSpec(block, lambda i, k, r, p: (i, k, 0, 0, 0)),
            scratch_shapes=[pltpu.VMEM((LANES, width), f32)] * 8,
        ),
        out_shape=jax.ShapeDtypeStruct((n, 4, 4, SUM_ROWS, width), f32),
        compiler_params=pltpu.CompilerParams(vmem_limit_bytes=32 * 2**20),
        name="partial_sums",
    )(*operands)


def split_sum_kernel(*refs):
    pieces, outs = refs[:4], refs[4:]
    for i in range(4):
        outs[i][...] = (pieces[0][i] + pieces[1][i]) + (pieces[2][i] + pieces[3][i])


def split_sums(pieces, name):
    return pl.pallas_call(
        split_sum_kernel,
        out_shape=[jax.ShapeDtypeStruct(pieces[0].shape[1:], f32)] * 4,
        compiler_params=pltpu.CompilerParams(vmem_limit_bytes=40 * 2**20),
        name=name,
    )(*pieces)


def along(stage, by):
    pairs = []
    for device in range(128):
        at = [device // 32, device // 16 % 2, device // 4 % 4, device % 4]
        axis = ORDERS[at[1]][stage]
        at[axis] = (at[axis] + by) % 4
        pairs.append((device, ((at[0] * 2 + at[1]) * 4 + at[2]) * 4 + at[3]))
    return pairs


def shifted(array, stage, by):
    return lax.ppermute(array, DP_ROWS, along(stage, by)) if by else array


def plane_of(core):
    here = jnp.stack([lax.axis_index(axis) for axis in DP_ROWS]).astype(i32)
    strides = jnp.array([32, 16, 4, 1], i32)
    orders = [jnp.array(order, i32) for order in ORDERS]
    order = jnp.where(core == 0, orders[0], orders[1])
    chosen = order[:, None] == jnp.arange(4, dtype=i32)[None, :]
    at = jnp.sum(jnp.where(chosen, here[None, :], 0), axis=1)
    stride = jnp.sum(jnp.where(chosen, strides[None, :], 0), axis=1)
    return jnp.concatenate([(core * 16)[None], at, stride])


def swapped(array):
    return lax.ppermute(array, CORE, [(0, 1), (1, 0)])


def to_sources(rows_idx, own, other, table, codes):
    received = []
    for firsts in ((1, 3), (2, 0)):
        mine = partial_sums(rows_idx, other, table, codes, firsts)
        received.append(swapped(mine))
    pieces = [None] * 4
    for k, first in enumerate((1, 3, 2, 0)):
        block = partial_sums(
            rows_idx, own, table, codes, (first,), received[k // 2], k % 2
        )
        pieces[first] = shifted(block.reshape(block.shape[1:]), 0, first)
    for stage in (1, 2):
        parts = split_sums(pieces, f"sum_stage_{stage}")
        pieces = [shifted(part, stage, by) for by, part in enumerate(parts)]
    return pieces


def user_kernel(*refs, hist_len, coef):
    item_ref, out_ref = refs[4:]
    sums = (refs[0][...] + refs[1][...]) + (refs[2][...] + refs[3][...])
    user = sums[:LANES] / hist_len
    positive = sums[LANES:]
    gap = jnp.sum(user * positive, axis=1, keepdims=True) - 1.0
    grad = 2.0 * gap * positive + 2.0 * coef * dot_split(user, item_ref[...])
    sq = (LANES, LANES)
    gap_row = jnp.sum(
        jnp.where(iota2(sq, 0) == iota2(sq, 1), jnp.broadcast_to(gap, sq), 0.0),
        axis=0,
        keepdims=True,
    )
    out_ref[:LANES, :] = grad / hist_len
    out_ref[LANES : 2 * LANES, :] = user
    out_ref[2 * LANES :, :] = jnp.broadcast_to(gap_row, (8, LANES))


def user_block(pieces, item_total, hist_len, coef):
    return pl.pallas_call(
        functools.partial(user_kernel, hist_len=hist_len, coef=coef),
        out_shape=jax.ShapeDtypeStruct((BLOCK_ROWS, pieces[0].shape[-1]), f32),
        name="user_block",
    )(*pieces, item_total)


def stack_kernel(*refs):
    for k in range(4):
        refs[4][k] = refs[k][...]


def stacked(pieces):
    return pl.pallas_call(
        stack_kernel,
        out_shape=jax.ShapeDtypeStruct((4,) + pieces[0].shape, f32),
        compiler_params=pltpu.CompilerParams(vmem_limit_bytes=24 * 2**20),
        name="stack_blocks",
    )(*pieces)


def update_kernel(
    row_idx_ref, code_idx_ref, planes_ref, *refs, sides, first, last, coef
):
    n = len(sides)
    blocks, refs = refs[:n], refs[n:]
    if not first:
        (carry_ref, carry_gram_ref), refs = refs[:2], refs[2:]
    if last:
        (table_ref, state_ref), refs = refs[:2], refs[2:]
    outs, refs = refs[:2], refs[2:]
    stage_ref, gram_ref, acc_refs = refs[0], refs[1], refs[2:]
    g = pl.program_id(0)
    sq = (LANES, LANES)
    rows_all = acc_refs[0].shape[0]

    @pl.when(g == 0)
    def _():
        for k, acc in enumerate(acc_refs):
            if k or first:
                acc[...] = jnp.zeros_like(acc)
            else:
                acc[...] = carry_ref[...]
        gram_ref[...] = jnp.zeros_like(gram_ref) if first else carry_gram_ref[...]

    diagonal = iota2(sq, 0) == iota2(sq, 1)
    for a in range(n):
        users = []
        for k in range(8):
            at = (8 * a + k) * 2 * LANES
            spot = (k // 4, k % 4)
            user = blocks[a][(*spot, slice(LANES, 2 * LANES))]
            gap_row = blocks[a][(*spot, slice(2 * LANES, 2 * LANES + 1))]
            gap = 2.0 * jnp.sum(
                jnp.where(diagonal, jnp.broadcast_to(gap_row, sq), 0.0), axis=1, keepdims=True
            )
            stage_ref[at : at + LANES, :] = blocks[a][(*spot, slice(0, LANES))]
            stage_ref[at + LANES : at + 2 * LANES, :] = gap * user
            users.append(user)
        gram_ref[...] += half_gram(jnp.concatenate(users, axis=0))

    for a, (side, offset) in enumerate(sides):
        here = [planes_ref[7 * side + k] for k in range(7)]
        base = here[0] + ((here[1] - offset) & 3) * here[4]

        def body(k, carry, a=a, here=here, base=base):
            at_second = ((here[2] - (2 * g + lax.shift_right_logical(k, 2))) & 3) * here[5]
            at_third = ((here[3] - (k & 3)) & 3) * here[6]
            source = (base + at_second + at_third) * LANES
            stage = (8 * a + k) * (2 * LANES)
            for at in range(0, LANES, CHAINS):
                rows = [row_idx_ref[source + (at + c)] for c in range(CHAINS)]
                srcs = [stage + code_idx_ref[source + (at + c)] for c in range(CHAINS)]
                grads = [stage_ref[pl.ds(srcs[c], 1), :] for c in range(CHAINS)]
                sums = [acc_refs[c][pl.ds(rows[c], 1), :] + grads[c] for c in range(CHAINS)]
                for c in range(CHAINS):
                    acc_refs[c][pl.ds(rows[c], 1), :] = sums[c]
            return carry

        lax.fori_loop(0, 8, body, 0)

    @pl.when(g == pl.num_programs(0) - 1)
    def _():
        if not last:
            total = acc_refs[0][...]
            for acc in acc_refs[1:]:
                total = total + acc[...]
            outs[0][...] = total
            outs[1][...] = gram_ref[...]
            return
        step = 512
        gram = whole_gram(gram_ref[...])

        def finish(i, carry):
            at = pl.ds(pl.multiple_of(i * step, step), step)
            table = table_ref[at, :]
            grad = 2.0 * coef * dot_split(table, gram)
            for acc in acc_refs:
                grad = grad + acc[at, :]
            new_state = state_ref[at, :] + grad * grad
            outs[1][at, :] = new_state
            outs[0][at, :] = table - step_size * grad / jnp.sqrt(new_state)
            return carry

        lax.fori_loop(0, (rows_all - 8) // step, finish, 0)


def update_rows(row_idx, code_idx, planes, blocks, sides, rows_dev, carry, final, coef):
    width = blocks[0].shape[-1]

    def whole(shape):
        return pl.BlockSpec(shape, lambda g, r, c, p: (0,) * len(shape))

    part = pl.BlockSpec((2, 4, BLOCK_ROWS, width), lambda g, r, c, p: (g, 0, 0, 0))
    extra = (*carry, *final)
    if final:
        out_shapes = [(rows_dev, width)] * 2
    else:
        out_shapes = [(rows_dev + 8, width), (width, 2 * width)]
    return pl.pallas_call(
        functools.partial(
            update_kernel, sides=sides, first=not carry, last=bool(final), coef=coef
        ),
        grid_spec=pltpu.PrefetchScalarGridSpec(
            num_scalar_prefetch=3,
            grid=(2,),
            in_specs=[part] * len(blocks) + [whole(array.shape) for array in extra],
            out_specs=[whole(shape) for shape in out_shapes],
            scratch_shapes=[
                pltpu.VMEM((len(blocks) * 8 * 2 * LANES, width), f32),
                pltpu.VMEM((width, 2 * width), f32),
            ]
            + [pltpu.VMEM((rows_dev + 8, width), f32)] * CHAINS,
        ),
        out_shape=[jax.ShapeDtypeStruct(shape, f32) for shape in out_shapes],
        compiler_params=pltpu.CompilerParams(vmem_limit_bytes=48 * 2**20),
        name="update_rows" if final else "add_rows",
    )(row_idx, code_idx, planes, *blocks, *extra)


def shards(item_table, adagrad_state, history_ids, positive_ids):
    rows_dev, width = item_table.shape
    _, hist_len = history_ids.shape
    devices = lax.axis_size(DP_ROWS)
    coef = penalty_weight / (rows_dev * devices)
    item_gram = jnp.dot(
        item_table.T,
        item_table,
        precision=lax.Precision.HIGHEST,
        preferred_element_type=f32,
    )
    lists = request_lists(history_ids, positive_ids, item_gram, rows_dev)
    asked = lax.all_to_all(lists, DP_ROWS, split_axis=0, concat_axis=0, tiled=True)
    rows = asked[:, 0, :].astype(i32).reshape(-1)
    codes = asked[:, 1, :]
    code_idx = jnp.maximum(codes.astype(i32).reshape(-1), 0)
    total_row = jnp.broadcast_to(asked[:, 2, :].sum(axis=0), (TOTAL_COPIES, width))
    total_row = lax.optimization_barrier(total_row)
    totals = lax.optimization_barrier(lax.all_gather(total_row, DP_ROWS))
    item_total = totals[:, 0, :]
    core = lax.axis_index(CORE).astype(i32)
    own, other = plane_of(core), plane_of(1 - core)
    planes = jnp.concatenate([own, other])
    pieces = to_sources(jnp.where(rows < rows_dev, rows, 0), own, other, item_table, codes)
    block = user_block(pieces, item_total, hist_len, coef)
    line = stacked([shifted(block, 2, by) for by in range(4)])
    plane = stacked([shifted(line, 1, by) for by in range(4)])
    update = functools.partial(update_rows, rows, code_idx, planes)
    near = (shifted(plane, 0, 1), shifted(plane, 0, 3))
    carry = update([plane, swapped(plane)], ((0, 0), (1, 0)), rows_dev, (), (), coef)
    plane, *near, carry = lax.optimization_barrier((plane, *near, carry))
    across = shifted(plane, 0, 2)
    carry = update(
        [*near, *map(swapped, near)], ((0, 1), (0, 3), (1, 1), (1, 3)), rows_dev, carry, (), coef
    )
    across, carry = lax.optimization_barrier((across, carry))
    return tuple(
        update(
            [across, swapped(across)],
            ((0, 2), (1, 2)),
            rows_dev,
            carry,
            (item_table, adagrad_state),
            coef,
        )
    )


def solution(mesh):
    finer = Mesh(mesh.devices.reshape(4, 2, 4, 4), DP_ROWS)
    rows = P(DP_ROWS, None)
    return jax.shard_map(
        shards,
        mesh=finer,
        in_specs=(rows, rows, rows, P(DP_ROWS)),
        out_specs=(rows, rows),
        check_vma=False,
    )
```

```python
import functools

import jax
import jax.numpy as jnp
from jax import lax
from jax.experimental import pallas as pl
from jax.experimental.pallas import tpu as pltpu
from jax.sharding import Mesh
from jax.sharding import PartitionSpec as P

X, CORE, Z, Y = "x", "core", "z", "y"
DP_ROWS = (X, CORE, Z, Y)
ORDERS = ((0, 2, 3), (2, 3, 0))

penalty_weight = 10.0
step_size = 0.05

LANES = 128
SUM_ROWS = 256
BLOCK_ROWS = 264
TOTAL_COPIES = 16
GROUP = 4
CHAINS = 4

bf16 = jnp.bfloat16
f32 = jnp.float32
i32 = jnp.int32


def iota2(shape, dim):
    return lax.broadcasted_iota(i32, shape, dim)


def split2(x):
    hi = x.astype(bf16)
    lo = (x - hi.astype(f32)).astype(bf16)
    return hi, lo


def dot_f32(a, b):
    return jnp.dot(a, b, preferred_element_type=f32)


def dot_split(a, b):
    ah, al = split2(a)
    bh, bl = split2(b)
    return dot_f32(ah, bh) + (dot_f32(ah, bl) + dot_f32(al, bh))


def half_gram(a):
    hi, lo = split2(a)
    return lax.dot_general(
        hi,
        jnp.concatenate([hi, lo], axis=1),
        (((0,), (0,)), ((), ())),
        preferred_element_type=f32,
    )


def whole_gram(halves):
    cross = halves[:, LANES:]
    return halves[:, :LANES] + (cross + cross.T)


def list_kernel(history_ref, positive_ref, table_ref, out_ref, *, slots, rows_dev):
    shift = rows_dev.bit_length() - 1
    sq = (LANES, LANES)
    ids = jnp.concatenate(
        [history_ref[...], positive_ref[...], jnp.full((LANES - slots, LANES), -1, i32)], axis=0
    )
    owner_r = lax.shift_right_arithmetic(ids, shift)
    owner_c = owner_r.T
    local = ids & (rows_dev - 1)
    high_r = (lax.shift_right_logical(local, 6) + 1).astype(f32)
    low_r = (local & 63).astype(f32)
    users = iota2((1, LANES), 1).astype(f32)
    lane = iota2(sq, 1)
    sub = iota2(sq, 0)
    lane_f = lane.astype(f32)
    one = jnp.ones(sq, f32)
    zero = jnp.zeros(sq, f32)
    lower = jnp.concatenate([jnp.where(sub > lane, one, zero), one], axis=0).astype(bf16)
    ones = one.astype(bf16)
    carry = jnp.zeros(sq, f32)
    acc = jnp.zeros((3 * LANES, LANES), f32)
    halves = jnp.zeros((LANES, 2 * LANES), f32)
    for at in range(0, rows_dev, 1024):
        halves = halves + half_gram(table_ref[at : at + 1024, :])
    for start in range(0, slots, GROUP):
        group = range(start, start + GROUP)
        members = [owner_c[:, h : h + 1] == lane for h in group]
        counts = dot_f32(
            lower,
            jnp.concatenate([jnp.where(m, one, zero) for m in members], axis=1).astype(bf16),
        )
        mine = []
        for k, member in enumerate(members):
            block = counts[:, k * LANES : (k + 1) * LANES]
            mine.append(jnp.where(member, block[:LANES] + carry, zero))
            carry = carry + block[LANES:]
        rank = dot_f32(jnp.concatenate(mine, axis=0).astype(bf16), ones)
        place = jnp.where(rank == jnp.concatenate([lane_f] * GROUP, axis=0), 1.0, 0.0)
        vals = []
        for h in group:
            at_owner = owner_r[h : h + 1, :] == sub
            code = users + (LANES if h == slots - 1 else 0)
            vals.append(
                jnp.concatenate(
                    [
                        jnp.where(at_owner, jnp.broadcast_to(value, sq), zero)
                        for value in (high_r[h : h + 1, :], low_r[h : h + 1, :], code)
                    ],
                    axis=0,
                )
            )
        acc = acc + dot_f32(jnp.concatenate(vals, axis=1).astype(bf16), place.astype(bf16))
    high = acc[:LANES].astype(i32)
    low = acc[LANES : 2 * LANES].astype(i32)
    code = acc[2 * LANES :].astype(i32)
    present = high > 0
    out_ref[:, 0, :] = jnp.where(present, (high - 1) * 64 + low, rows_dev).astype(f32)
    out_ref[:, 1, :] = jnp.where(present, code, -1).astype(f32)
    out_ref[:, 2, :] = whole_gram(halves)
    out_ref[:, 3, :] = zero


def request_lists(history_ids, positive_ids, table):
    rows_dev = table.shape[0]
    users, hist_len = history_ids.shape
    return pl.pallas_call(
        functools.partial(list_kernel, slots=hist_len + 1, rows_dev=rows_dev),
        out_shape=jax.ShapeDtypeStruct((LANES, 4, LANES), f32),
        compiler_params=pltpu.CompilerParams(vmem_limit_bytes=16 * 2**20),
        name="request_lists",
    )(history_ids.T, positive_ids.reshape(1, users), table)


def partial_kernel(rows_ref, plane_ref, table_ref, codes_ref, *refs, first, first_step):
    from_ref = refs[0] if len(refs) == 10 else None
    out_ref = refs[-9]
    picked_refs = refs[-8:]
    code_of = iota2((2 * LANES, LANES), 0).astype(f32)
    one = jnp.ones((2 * LANES, LANES), f32)
    zero = jnp.zeros((2 * LANES, LANES), f32)
    unroll = 32
    offsets = (first + first_step * pl.program_id(0), 2 * pl.program_id(1))
    at_first = ((plane_ref[1] + offsets[0]) & 3) * plane_ref[4]
    for k in range(2):
        at_second = ((plane_ref[2] + (offsets[1] + k)) & 3) * plane_ref[5]
        for j in range(4):
            at_third = ((plane_ref[3] + j) & 3) * plane_ref[6]
            source = plane_ref[0] + at_first + at_second + at_third
            base = source * LANES
            picked_ref = picked_refs[4 * k + j]
            for at in range(0, LANES, unroll):
                picked = [
                    table_ref[pl.ds(rows_ref[base + (at + i)], 1), :] for i in range(unroll)
                ]
                for i in range(unroll):
                    picked_ref[at + i : at + i + 1, :] = picked[i]
            weight = jnp.where(codes_ref[pl.ds(source, 1), :] == code_of, one, zero)
            weight = weight.astype(bf16)
            block = dot_f32(
                jnp.concatenate([weight, weight], axis=1),
                jnp.concatenate(split2(picked_ref[...]), axis=0),
            )
            if from_ref is not None:
                block = block + from_ref[0, k, j]
            out_ref[0, k, j] = block


def partial_sums(rows_idx, plane, table, codes, firsts, received=None, place=0):
    rows_dev, width = table.shape
    n = len(firsts)
    block = (1, 2, 4, SUM_ROWS, width)

    def whole(shape):
        return pl.BlockSpec(shape, lambda i, k, r, p: (0,) * len(shape))

    in_specs = [whole((rows_dev, width)), whole(codes.shape)]
    operands = (rows_idx, plane, table, codes)
    if received is not None:
        in_specs.append(pl.BlockSpec(block, lambda i, k, r, p: (place, k, 0, 0, 0)))
        operands += (received,)
    return pl.pallas_call(
        functools.partial(
            partial_kernel, first=firsts[0], first_step=firsts[-1] - firsts[0]
        ),
        grid_spec=pltpu.PrefetchScalarGridSpec(
            num_scalar_prefetch=2,
            grid=(n, 2),
            in_specs=in_specs,
            out_specs=pl.BlockSpec(block, lambda i, k, r, p: (i, k, 0, 0, 0)),
            scratch_shapes=[pltpu.VMEM((LANES, width), f32)] * 8,
        ),
        out_shape=jax.ShapeDtypeStruct((n, 4, 4, SUM_ROWS, width), f32),
        compiler_params=pltpu.CompilerParams(vmem_limit_bytes=24 * 2**20),
        name="partial_sums",
    )(*operands)


def split_sum_kernel(*refs):
    pieces, outs = refs[:4], refs[4:]
    for i in range(4):
        outs[i][...] = (pieces[0][i] + pieces[1][i]) + (pieces[2][i] + pieces[3][i])


def split_sums(pieces, name):
    return pl.pallas_call(
        split_sum_kernel,
        out_shape=[jax.ShapeDtypeStruct(pieces[0].shape[1:], f32)] * 4,
        compiler_params=pltpu.CompilerParams(vmem_limit_bytes=24 * 2**20),
        name=name,
    )(*pieces)


def along(stage, by):
    pairs = []
    for device in range(128):
        at = [device // 32, device // 16 % 2, device // 4 % 4, device % 4]
        axis = ORDERS[at[1]][stage]
        at[axis] = (at[axis] + by) % 4
        pairs.append((device, ((at[0] * 2 + at[1]) * 4 + at[2]) * 4 + at[3]))
    return pairs


def shifted(array, stage, by):
    return lax.ppermute(array, DP_ROWS, along(stage, by)) if by else array


def plane_of(core):
    here = jnp.stack([lax.axis_index(axis) for axis in DP_ROWS]).astype(i32)
    strides = jnp.array([32, 16, 4, 1], i32)
    orders = [jnp.array(order, i32) for order in ORDERS]
    order = jnp.where(core == 0, orders[0], orders[1])
    chosen = order[:, None] == jnp.arange(4, dtype=i32)[None, :]
    at = jnp.sum(jnp.where(chosen, here[None, :], 0), axis=1)
    stride = jnp.sum(jnp.where(chosen, strides[None, :], 0), axis=1)
    return jnp.concatenate([(core * 16)[None], at, stride])


def swapped(array):
    return lax.ppermute(array, CORE, [(0, 1), (1, 0)])


def to_sources(rows_idx, own, other, table, codes):
    received = []
    for firsts in ((1, 3), (2, 0)):
        mine = partial_sums(rows_idx, other, table, codes, firsts)
        received.append(swapped(mine))
    pieces = [None] * 4
    for k, first in enumerate((1, 3, 2, 0)):
        block = partial_sums(
            rows_idx, own, table, codes, (first,), received[k // 2], k % 2
        )
        pieces[first] = shifted(block.reshape(block.shape[1:]), 0, first)
    for stage in (1, 2):
        parts = split_sums(pieces, f"sum_stage_{stage}")
        pieces = [shifted(part, stage, by) for by, part in enumerate(parts)]
    return pieces


def user_kernel(*refs, hist_len, coef):
    item_ref, out_ref = refs[4:]
    sums = (refs[0][...] + refs[1][...]) + (refs[2][...] + refs[3][...])
    user = sums[:LANES] / hist_len
    positive = sums[LANES:]
    gap = jnp.sum(user * positive, axis=1, keepdims=True) - 1.0
    grad = 2.0 * gap * positive + 2.0 * coef * dot_split(user, item_ref[...])
    sq = (LANES, LANES)
    gap_row = jnp.sum(
        jnp.where(iota2(sq, 0) == iota2(sq, 1), jnp.broadcast_to(gap, sq), 0.0),
        axis=0,
        keepdims=True,
    )
    out_ref[:LANES, :] = grad / hist_len
    out_ref[LANES : 2 * LANES, :] = user
    out_ref[2 * LANES :, :] = jnp.broadcast_to(gap_row, (8, LANES))


def user_block(pieces, item_total, hist_len, coef):
    return pl.pallas_call(
        functools.partial(user_kernel, hist_len=hist_len, coef=coef),
        out_shape=jax.ShapeDtypeStruct((BLOCK_ROWS, pieces[0].shape[-1]), f32),
        name="user_block",
    )(*pieces, item_total)


def stack_kernel(*refs):
    for k in range(4):
        refs[4][k] = refs[k][...]


def stacked(pieces):
    return pl.pallas_call(
        stack_kernel,
        out_shape=jax.ShapeDtypeStruct((4,) + pieces[0].shape, f32),
        compiler_params=pltpu.CompilerParams(vmem_limit_bytes=24 * 2**20),
        name="stack_blocks",
    )(*pieces)


def update_kernel(
    row_idx_ref, code_idx_ref, planes_ref, *refs, sides, first, last, coef
):
    n = len(sides)
    blocks, refs = refs[:n], refs[n:]
    if not first:
        (carry_ref, carry_gram_ref), refs = refs[:2], refs[2:]
    if last:
        (table_ref, state_ref), refs = refs[:2], refs[2:]
    outs, refs = refs[:2], refs[2:]
    stage_ref, gram_ref, acc_refs = refs[0], refs[1], refs[2:]
    g = pl.program_id(0)
    sq = (LANES, LANES)
    rows_all = acc_refs[0].shape[0]

    @pl.when(g == 0)
    def _():
        for k, acc in enumerate(acc_refs):
            if k or first:
                acc[...] = jnp.zeros_like(acc)
            else:
                acc[...] = carry_ref[...]
        gram_ref[...] = jnp.zeros_like(gram_ref) if first else carry_gram_ref[...]

    diagonal = iota2(sq, 0) == iota2(sq, 1)
    for a in range(n):
        users = []
        for k in range(8):
            at = (8 * a + k) * 2 * LANES
            spot = (k // 4, k % 4)
            user = blocks[a][(*spot, slice(LANES, 2 * LANES))]
            gap_row = blocks[a][(*spot, slice(2 * LANES, 2 * LANES + 1))]
            gap = 2.0 * jnp.sum(
                jnp.where(diagonal, jnp.broadcast_to(gap_row, sq), 0.0), axis=1, keepdims=True
            )
            stage_ref[at : at + LANES, :] = blocks[a][(*spot, slice(0, LANES))]
            stage_ref[at + LANES : at + 2 * LANES, :] = gap * user
            users.append(user)
        gram_ref[...] += half_gram(jnp.concatenate(users, axis=0))

    for a, (side, offset) in enumerate(sides):
        here = [planes_ref[7 * side + k] for k in range(7)]
        base = here[0] + ((here[1] - offset) & 3) * here[4]

        def body(k, carry, a=a, here=here, base=base):
            at_second = ((here[2] - (2 * g + lax.shift_right_logical(k, 2))) & 3) * here[5]
            at_third = ((here[3] - (k & 3)) & 3) * here[6]
            source = (base + at_second + at_third) * LANES
            stage = (8 * a + k) * (2 * LANES)
            for at in range(0, LANES, CHAINS):
                rows = [row_idx_ref[source + (at + c)] for c in range(CHAINS)]
                srcs = [stage + code_idx_ref[source + (at + c)] for c in range(CHAINS)]
                grads = [stage_ref[pl.ds(srcs[c], 1), :] for c in range(CHAINS)]
                sums = [acc_refs[c][pl.ds(rows[c], 1), :] + grads[c] for c in range(CHAINS)]
                for c in range(CHAINS):
                    acc_refs[c][pl.ds(rows[c], 1), :] = sums[c]
            return carry

        lax.fori_loop(0, 8, body, 0)

    @pl.when(g == pl.num_programs(0) - 1)
    def _():
        if not last:
            total = acc_refs[0][...]
            for acc in acc_refs[1:]:
                total = total + acc[...]
            outs[0][...] = total
            outs[1][...] = gram_ref[...]
            return
        step = 512
        gram = whole_gram(gram_ref[...])

        def finish(i, carry):
            at = pl.ds(pl.multiple_of(i * step, step), step)
            table = table_ref[at, :]
            grad = 2.0 * coef * dot_split(table, gram)
            for acc in acc_refs:
                grad = grad + acc[at, :]
            new_state = state_ref[at, :] + grad * grad
            outs[1][at, :] = new_state
            outs[0][at, :] = table - step_size * grad / jnp.sqrt(new_state)
            return carry

        lax.fori_loop(0, (rows_all - 8) // step, finish, 0)


def update_rows(row_idx, code_idx, planes, blocks, sides, rows_dev, carry, final, coef):
    width = blocks[0].shape[-1]

    def whole(shape):
        return pl.BlockSpec(shape, lambda g, r, c, p: (0,) * len(shape))

    part = pl.BlockSpec((2, 4, BLOCK_ROWS, width), lambda g, r, c, p: (g, 0, 0, 0))
    extra = (*carry, *final)
    if final:
        out_shapes = [(rows_dev, width)] * 2
    else:
        out_shapes = [(rows_dev + 8, width), (width, 2 * width)]
    return pl.pallas_call(
        functools.partial(
            update_kernel, sides=sides, first=not carry, last=bool(final), coef=coef
        ),
        grid_spec=pltpu.PrefetchScalarGridSpec(
            num_scalar_prefetch=3,
            grid=(2,),
            in_specs=[part] * len(blocks) + [whole(array.shape) for array in extra],
            out_specs=[whole(shape) for shape in out_shapes],
            scratch_shapes=[
                pltpu.VMEM((len(blocks) * 8 * 2 * LANES, width), f32),
                pltpu.VMEM((width, 2 * width), f32),
            ]
            + [pltpu.VMEM((rows_dev + 8, width), f32)] * CHAINS,
        ),
        out_shape=[jax.ShapeDtypeStruct(shape, f32) for shape in out_shapes],
        compiler_params=pltpu.CompilerParams(vmem_limit_bytes=48 * 2**20),
        name="update_rows" if final else "add_rows",
    )(row_idx, code_idx, planes, *blocks, *extra)


def shards(item_table, adagrad_state, history_ids, positive_ids):
    rows_dev, width = item_table.shape
    _, hist_len = history_ids.shape
    devices = lax.axis_size(DP_ROWS)
    coef = penalty_weight / (rows_dev * devices)
    lists = request_lists(history_ids, positive_ids, item_table)
    asked = lax.all_to_all(lists, DP_ROWS, split_axis=0, concat_axis=0, tiled=True)
    rows = asked[:, 0, :].astype(i32).reshape(-1)
    codes = asked[:, 1, :]
    code_idx = jnp.maximum(codes.astype(i32).reshape(-1), 0)
    total_row = jnp.broadcast_to(asked[:, 2, :].sum(axis=0), (TOTAL_COPIES, width))
    total_row = lax.optimization_barrier(total_row)
    totals = lax.optimization_barrier(lax.all_gather(total_row, DP_ROWS))
    item_total = totals[:, 0, :]
    core = lax.axis_index(CORE).astype(i32)
    own, other = plane_of(core), plane_of(1 - core)
    planes = jnp.concatenate([own, other])
    pieces = to_sources(jnp.where(rows < rows_dev, rows, 0), own, other, item_table, codes)
    block = user_block(pieces, item_total, hist_len, coef)
    line = stacked([shifted(block, 2, by) for by in range(4)])
    plane = stacked([shifted(line, 1, by) for by in range(4)])
    update = functools.partial(update_rows, rows, code_idx, planes)
    near = (shifted(plane, 0, 1), shifted(plane, 0, 3))
    carry = update([plane, swapped(plane)], ((0, 0), (1, 0)), rows_dev, (), (), coef)
    plane, *near, carry = lax.optimization_barrier((plane, *near, carry))
    across = shifted(plane, 0, 2)
    far = [swapped(piece) for piece in near]
    carry = update(near, ((0, 1), (0, 3)), rows_dev, carry, (), coef)
    *far, carry = lax.optimization_barrier((*far, carry))
    carry = update(far, ((1, 1), (1, 3)), rows_dev, carry, (), coef)
    across, carry = lax.optimization_barrier((across, carry))
    return tuple(
        update(
            [across, swapped(across)],
            ((0, 2), (1, 2)),
            rows_dev,
            carry,
            (item_table, adagrad_state),
            coef,
        )
    )


def solution(mesh):
    finer = Mesh(mesh.devices.reshape(4, 2, 4, 4), DP_ROWS)
    rows = P(DP_ROWS, None)
    return jax.shard_map(
        shards,
        mesh=finer,
        in_specs=(rows, rows, rows, P(DP_ROWS)),
        out_specs=(rows, rows),
        check_vma=False,
    )
```

```python
import functools

import jax
import jax.numpy as jnp
from jax import lax
from jax.experimental import pallas as pl
from jax.experimental.pallas import tpu as pltpu
from jax.sharding import Mesh
from jax.sharding import PartitionSpec as P

X, CORE, Z, Y = "x", "core", "z", "y"
DP_ROWS = (X, CORE, Z, Y)
ORDERS = ((0, 2, 3), (2, 3, 0))

penalty_weight = 10.0
step_size = 0.05

LANES = 128
BLOCK_ROWS = 264
GROUP = 4
CHAINS = 4

bf16 = jnp.bfloat16
f32 = jnp.float32
i32 = jnp.int32


def iota2(shape, dim):
    return lax.broadcasted_iota(i32, shape, dim)


def split2(x):
    hi = x.astype(bf16)
    lo = (x - hi.astype(f32)).astype(bf16)
    return hi, lo


def dot_f32(a, b):
    return jnp.dot(a, b, preferred_element_type=f32)


def dot_split(a, b):
    ah, al = split2(a)
    bh, bl = split2(b)
    return dot_f32(ah, bh) + (dot_f32(ah, bl) + dot_f32(al, bh))


def half_gram(a):
    hi, lo = split2(a)
    return lax.dot_general(
        hi,
        jnp.concatenate([hi, lo], axis=1),
        (((0,), (0,)), ((), ())),
        preferred_element_type=f32,
    )


def whole_gram(halves):
    cross = halves[:, LANES:]
    return halves[:, :LANES] + (cross + cross.T)


def list_kernel(history_ref, positive_ref, out_ref, *, slots, rows_dev):
    shift = rows_dev.bit_length() - 1
    sq = (LANES, LANES)
    ids = jnp.concatenate(
        [history_ref[...], positive_ref[...], jnp.full((LANES - slots, LANES), -1, i32)], axis=0
    )
    owner_r = lax.shift_right_arithmetic(ids, shift)
    owner_c = owner_r.T
    local = ids & (rows_dev - 1)
    high_r = (lax.shift_right_logical(local, 6) + 1).astype(f32)
    low_r = (local & 63).astype(f32)
    users = iota2((1, LANES), 1).astype(f32)
    lane = iota2(sq, 1)
    sub = iota2(sq, 0)
    lane_f = lane.astype(f32)
    one = jnp.ones(sq, f32)
    zero = jnp.zeros(sq, f32)
    lower = jnp.concatenate([jnp.where(sub > lane, one, zero), one], axis=0).astype(bf16)
    ones = one.astype(bf16)
    carry = jnp.zeros(sq, f32)
    acc = jnp.zeros((3 * LANES, LANES), f32)
    for start in range(0, slots, GROUP):
        group = range(start, start + GROUP)
        members = [owner_c[:, h : h + 1] == lane for h in group]
        counts = dot_f32(
            lower,
            jnp.concatenate([jnp.where(m, one, zero) for m in members], axis=1).astype(bf16),
        )
        mine = []
        for k, member in enumerate(members):
            block = counts[:, k * LANES : (k + 1) * LANES]
            mine.append(jnp.where(member, block[:LANES] + carry, zero))
            carry = carry + block[LANES:]
        rank = dot_f32(jnp.concatenate(mine, axis=0).astype(bf16), ones)
        place = jnp.where(rank == jnp.concatenate([lane_f] * GROUP, axis=0), 1.0, 0.0)
        vals = []
        for h in group:
            at_owner = owner_r[h : h + 1, :] == sub
            code = users + (LANES if h == slots - 1 else 0)
            vals.append(
                jnp.concatenate(
                    [
                        jnp.where(at_owner, jnp.broadcast_to(value, sq), zero)
                        for value in (high_r[h : h + 1, :], low_r[h : h + 1, :], code)
                    ],
                    axis=0,
                )
            )
        acc = acc + dot_f32(jnp.concatenate(vals, axis=1).astype(bf16), place.astype(bf16))
    high = acc[:LANES].astype(i32)
    low = acc[LANES : 2 * LANES].astype(i32)
    code = acc[2 * LANES :].astype(i32)
    present = high > 0
    out_ref[:, 0, :] = jnp.where(present, (high - 1) * 64 + low, rows_dev).astype(f32)
    out_ref[:, 1, :] = jnp.where(present, code, -1).astype(f32)


def request_lists(history_ids, positive_ids, rows_dev):
    users, hist_len = history_ids.shape
    return pl.pallas_call(
        functools.partial(list_kernel, slots=hist_len + 1, rows_dev=rows_dev),
        out_shape=jax.ShapeDtypeStruct((LANES, 2, LANES), f32),
        name="request_lists",
    )(history_ids.T, positive_ids.reshape(1, users))


def partial_kernel(rows_ref, plane_ref, table_ref, codes_ref, gram_ref, *refs, first, first_step, takes):
    from_ref = refs[0] if takes else None
    out_refs = refs[int(takes) : -8]
    picked_refs = refs[-8:]
    code_of = iota2((2 * LANES, LANES), 0).astype(f32)
    one = jnp.ones((2 * LANES, LANES), f32)
    zero = jnp.zeros((2 * LANES, LANES), f32)
    unroll = 32
    offsets = (first + first_step * pl.program_id(0), 2 * pl.program_id(1))
    at_first = ((plane_ref[1] + offsets[0]) & 3) * plane_ref[4]
    for k in range(2):
        at_second = ((plane_ref[2] + (offsets[1] + k)) & 3) * plane_ref[5]
        for j in range(4):
            at_third = ((plane_ref[3] + j) & 3) * plane_ref[6]
            source = plane_ref[0] + at_first + at_second + at_third
            base = source * LANES
            picked_ref = picked_refs[4 * k + j]
            for at in range(0, LANES, unroll):
                picked = [
                    table_ref[pl.ds(rows_ref[base + (at + i)], 1), :] for i in range(unroll)
                ]
                for i in range(unroll):
                    picked_ref[at + i : at + i + 1, :] = picked[i]
            weight = jnp.where(codes_ref[pl.ds(source, 1), :] == code_of, one, zero)
            weight = weight.astype(bf16)
            block = dot_f32(
                jnp.concatenate([weight, weight], axis=1),
                jnp.concatenate(split2(picked_ref[...]), axis=0),
            )
            gram = jnp.broadcast_to(gram_ref[pl.ds(source, 1), :], (8, LANES))
            if from_ref is not None:
                block = block + from_ref[0, k, j, : 2 * LANES, :]
                gram = gram + from_ref[0, k, j, 2 * LANES :, :]
            if len(out_refs) == 2:
                out_refs[0][0, k, j] = block[:LANES]
                out_refs[1][0, k, j, :LANES, :] = block[LANES:]
                out_refs[1][0, k, j, LANES:, :] = gram
            else:
                out_refs[0][0, k, j, : 2 * LANES, :] = block
                out_refs[0][0, k, j, 2 * LANES :, :] = gram


def partial_sums(rows_idx, plane, table, codes, gram, firsts, received=None, place=0, split=False):
    rows_dev, width = table.shape
    n = len(firsts)
    block = (1, 2, 4, BLOCK_ROWS, width)
    sizes = (LANES, BLOCK_ROWS - LANES) if split else (BLOCK_ROWS,)

    def whole(shape):
        return pl.BlockSpec(shape, lambda i, k, r, p: (0,) * len(shape))

    in_specs = [whole((rows_dev, width)), whole(codes.shape), whole(gram.shape)]
    operands = (rows_idx, plane, table, codes, gram)
    if received is not None:
        in_specs.append(pl.BlockSpec(block, lambda i, k, r, p: (place, k, 0, 0, 0)))
        operands += (received,)
    return pl.pallas_call(
        functools.partial(
            partial_kernel,
            first=firsts[0],
            first_step=firsts[-1] - firsts[0],
            takes=received is not None,
        ),
        grid_spec=pltpu.PrefetchScalarGridSpec(
            num_scalar_prefetch=2,
            grid=(n, 2),
            in_specs=in_specs,
            out_specs=[
                pl.BlockSpec((1, 2, 4, size, width), lambda i, k, r, p: (i, k, 0, 0, 0))
                for size in sizes
            ],
            scratch_shapes=[pltpu.VMEM((LANES, width), f32)] * 8,
        ),
        out_shape=[jax.ShapeDtypeStruct((n, 4, 4, size, width), f32) for size in sizes],
        compiler_params=pltpu.CompilerParams(vmem_limit_bytes=32 * 2**20),
        name="partial_sums",
    )(*operands)


def split_sum_kernel(*refs):
    pieces, outs = refs[:-4], refs[-4:]
    for i in range(4):
        total = pieces[0][i]
        for piece in pieces[1:]:
            total = total + piece[i]
        outs[i][...] = total


def split_sums(pieces, name):
    return pl.pallas_call(
        split_sum_kernel,
        out_shape=[jax.ShapeDtypeStruct(pieces[0].shape[1:], f32)] * 4,
        compiler_params=pltpu.CompilerParams(vmem_limit_bytes=40 * 2**20),
        name=name,
    )(*pieces)


def add_rows_kernel(block_ref, part_ref, out_ref, *, start):
    end = start + part_ref.shape[2]
    for k in range(4):
        out_ref[k] = block_ref[k]
        out_ref[k, :, start:end, :] = block_ref[k, :, start:end, :] + part_ref[k]


def with_rows(block, part, start):
    return pl.pallas_call(
        functools.partial(add_rows_kernel, start=start),
        out_shape=jax.ShapeDtypeStruct(block.shape, f32),
        compiler_params=pltpu.CompilerParams(vmem_limit_bytes=24 * 2**20),
        name="add_relayed",
    )(block, part)


def along(stage, by):
    pairs = []
    for device in range(128):
        at = [device // 32, device // 16 % 2, device // 4 % 4, device % 4]
        axis = ORDERS[at[1]][stage]
        at[axis] = (at[axis] + by) % 4
        pairs.append((device, ((at[0] * 2 + at[1]) * 4 + at[2]) * 4 + at[3]))
    return pairs


def shifted(array, stage, by):
    return lax.ppermute(array, DP_ROWS, along(stage, by)) if by else array


def plane_of(core):
    here = jnp.stack([lax.axis_index(axis) for axis in DP_ROWS]).astype(i32)
    strides = jnp.array([32, 16, 4, 1], i32)
    orders = [jnp.array(order, i32) for order in ORDERS]
    order = jnp.where(core == 0, orders[0], orders[1])
    chosen = order[:, None] == jnp.arange(4, dtype=i32)[None, :]
    at = jnp.sum(jnp.where(chosen, here[None, :], 0), axis=1)
    stride = jnp.sum(jnp.where(chosen, strides[None, :], 0), axis=1)
    return jnp.concatenate([(core * 16)[None], at, stride])


def to_sources(rows_idx, table, codes, gram):
    core = lax.axis_index(CORE).astype(i32)
    other, own = plane_of(1 - core), plane_of(core)
    swap = [(0, 1), (1, 0)]
    received = []
    for firsts in ((1, 3), (2, 0)):
        (mine,) = partial_sums(rows_idx, other, table, codes, gram, firsts)
        received.append(lax.ppermute(mine, CORE, swap))

    def blocks(first, k, split=False):
        outs = partial_sums(
            rows_idx, own, table, codes, gram, (first,), received[k // 2], k % 2, split
        )
        return [out.reshape(out.shape[1:]) for out in outs]

    upper, lower = blocks(2, 2, True)
    upper, lower = shifted(upper, 0, 1), shifted(lower, 0, 3)
    (ahead,), (behind,), (here,) = blocks(1, 0), blocks(3, 1), blocks(0, 3)
    ahead = shifted(with_rows(ahead, upper, 0), 0, 1)
    behind = shifted(with_rows(behind, lower, LANES), 0, 3)
    pieces = [here, ahead, behind]
    for stage in (1, 2):
        parts = split_sums(pieces, f"sum_stage_{stage}")
        pieces = [shifted(part, stage, by) for by, part in enumerate(parts)]
    return pieces


def user_kernel(*refs, hist_len):
    out_ref = refs[4]
    sums = (refs[0][...] + refs[1][...]) + (refs[2][...] + refs[3][...])
    user = sums[:LANES] / hist_len
    positive = sums[LANES : 2 * LANES]
    gap = jnp.sum(user * positive, axis=1, keepdims=True) - 1.0
    sq = (LANES, LANES)
    gap_row = jnp.sum(
        jnp.where(iota2(sq, 0) == iota2(sq, 1), jnp.broadcast_to(gap, sq), 0.0),
        axis=0,
        keepdims=True,
    )
    out_ref[:LANES, :] = positive
    out_ref[LANES : 2 * LANES, :] = user
    tail = (8, LANES)
    out_ref[2 * LANES :, :] = jnp.where(
        iota2(tail, 0) == 0,
        jnp.broadcast_to(gap_row, tail),
        sums[2 * LANES :],
    )


def user_block(pieces, hist_len):
    return pl.pallas_call(
        functools.partial(user_kernel, hist_len=hist_len),
        out_shape=jax.ShapeDtypeStruct(pieces[0].shape, f32),
        name="user_block",
    )(*pieces)


def update_kernel(
    row_idx_ref, src_idx_ref, blocks_ref, item_ref, table_ref, state_ref, new_table_ref, new_state_ref,
    stage_ref, gram_ref, *acc_refs, sources, coef, hist_len,
):
    g = pl.program_id(0)
    rows_dev = table_ref.shape[0]
    sq = (LANES, LANES)

    @pl.when(g == 0)
    def _():
        gram_ref[...] = jnp.zeros_like(gram_ref)
        for acc in acc_refs:
            acc[...] = jnp.zeros_like(acc)

    diagonal = iota2(sq, 0) == iota2(sq, 1)
    users = jnp.concatenate(
        [blocks_ref[s, LANES : 2 * LANES, :] for s in range(sources)], axis=0
    )
    pulls = dot_split(users, item_ref[...])
    for s in range(sources):
        user = blocks_ref[s, LANES : 2 * LANES, :]
        gap_row = blocks_ref[s, 2 * LANES : 2 * LANES + 1, :]
        gap = 2.0 * jnp.sum(
            jnp.where(diagonal, jnp.broadcast_to(gap_row, sq), 0.0), axis=1, keepdims=True
        )
        pull = pulls[LANES * s : LANES * (s + 1)]
        grad = gap * blocks_ref[s, :LANES, :] + 2.0 * coef * pull
        stage_ref[2 * LANES * s : 2 * LANES * s + LANES, :] = grad / hist_len
        stage_ref[2 * LANES * s + LANES : 2 * LANES * (s + 1), :] = gap * user
    gram_ref[...] += half_gram(users)

    base = g * (sources * LANES)
    unroll = 128

    def body(j, carry):
        for at in range(0, unroll, CHAINS):
            first = base + j * unroll + at
            rows = [row_idx_ref[first + k] for k in range(CHAINS)]
            srcs = [src_idx_ref[first + k] for k in range(CHAINS)]
            grads = [stage_ref[pl.ds(srcs[k], 1), :] for k in range(CHAINS)]
            sums = [acc_refs[k][pl.ds(rows[k], 1), :] + grads[k] for k in range(CHAINS)]
            for k in range(CHAINS):
                acc_refs[k][pl.ds(rows[k], 1), :] = sums[k]
        return carry

    lax.fori_loop(0, sources * LANES // unroll, body, 0)

    @pl.when(g == pl.num_programs(0) - 1)
    def _():
        step = 512
        gram = whole_gram(gram_ref[...])

        def finish(i, carry):
            at = pl.ds(pl.multiple_of(i * step, step), step)
            table = table_ref[at, :]
            grad = 2.0 * coef * dot_split(table, gram)
            for acc in acc_refs:
                grad = grad + acc[at, :]
            new_state = state_ref[at, :] + grad * grad
            new_state_ref[at, :] = new_state
            new_table_ref[at, :] = table - step_size * grad / jnp.sqrt(new_state)
            return carry

        lax.fori_loop(0, rows_dev // step, finish, 0)


def update_rows(row_idx, src_idx, blocks, item_total, table, state, coef, hist_len):
    rows_dev, width = table.shape
    devices = blocks.shape[0]
    sources = 16
    whole = pl.BlockSpec((rows_dev, width), lambda g, r, s: (0, 0))
    return pl.pallas_call(
        functools.partial(update_kernel, sources=sources, coef=coef, hist_len=hist_len),
        grid_spec=pltpu.PrefetchScalarGridSpec(
            num_scalar_prefetch=2,
            grid=(devices // sources,),
            in_specs=[
                pl.BlockSpec((sources, BLOCK_ROWS, width), lambda g, r, s: (g, 0, 0)),
                pl.BlockSpec((width, width), lambda g, r, s: (0, 0)),
                whole,
                whole,
            ],
            out_specs=[whole, whole],
            scratch_shapes=[
                pltpu.VMEM((sources * 2 * LANES, width), f32),
                pltpu.VMEM((width, 2 * width), f32),
            ]
            + [pltpu.VMEM((rows_dev + 8, width), f32)] * CHAINS,
        ),
        out_shape=(
            jax.ShapeDtypeStruct((rows_dev, width), f32),
            jax.ShapeDtypeStruct((rows_dev, width), f32),
        ),
        compiler_params=pltpu.CompilerParams(vmem_limit_bytes=48 * 2**20),
        name="update_rows",
    )(row_idx, src_idx, blocks, item_total, table, state)


def shards(item_table, adagrad_state, history_ids, positive_ids):
    rows_dev, width = item_table.shape
    users_dev, hist_len = history_ids.shape
    devices = lax.axis_size(DP_ROWS)
    coef = penalty_weight / (rows_dev * devices)
    item_gram = jnp.dot(
        item_table.T,
        item_table,
        precision=lax.Precision.HIGHEST,
        preferred_element_type=f32,
    )
    lists = request_lists(history_ids, positive_ids, rows_dev)
    asked = lax.all_to_all(lists, DP_ROWS, split_axis=0, concat_axis=0, tiled=True)
    rows = asked[:, 0, :].astype(i32).reshape(-1)
    codes = asked[:, 1, :]
    place = jnp.arange(devices * LANES, dtype=i32) // LANES % 16 * (2 * LANES)
    src_idx = place + jnp.maximum(codes.astype(i32).reshape(-1), 0)
    pieces = to_sources(jnp.where(rows < rows_dev, rows, 0), item_table, codes, item_gram)
    block = user_block(pieces, hist_len)
    blocks = lax.all_gather(block, DP_ROWS)
    item_total = blocks[:, 2 * LANES + 1, :]
    return update_rows(
        rows, src_idx, blocks, item_total, item_table, adagrad_state, coef, hist_len
    )


def solution(mesh):
    finer = Mesh(mesh.devices.reshape(4, 2, 4, 4), DP_ROWS)
    rows = P(DP_ROWS, None)
    return jax.shard_map(
        shards,
        mesh=finer,
        in_specs=(rows, rows, rows, P(DP_ROWS)),
        out_specs=(rows, rows),
        check_vma=False,
    )
```

```python
import functools

import jax
import jax.numpy as jnp
from jax import lax
from jax.experimental import pallas as pl
from jax.experimental.pallas import tpu as pltpu
from jax.sharding import Mesh
from jax.sharding import PartitionSpec as P

X, CORE, Z, Y = "x", "core", "z", "y"
DP_ROWS = (X, CORE, Z, Y)
ORDERS = ((0, 2, 3), (2, 3, 0))

penalty_weight = 10.0
step_size = 0.05

LANES = 128
BLOCK_ROWS = 264
GROUP = 4
CHAINS = 4

bf16 = jnp.bfloat16
f32 = jnp.float32
i32 = jnp.int32


def iota2(shape, dim):
    return lax.broadcasted_iota(i32, shape, dim)


def split2(x):
    hi = x.astype(bf16)
    lo = (x - hi.astype(f32)).astype(bf16)
    return hi, lo


def dot_f32(a, b):
    return jnp.dot(a, b, preferred_element_type=f32)


def dot_split(a, b):
    ah, al = split2(a)
    bh, bl = split2(b)
    return dot_f32(ah, bh) + (dot_f32(ah, bl) + dot_f32(al, bh))


def half_gram(a):
    hi, lo = split2(a)
    return lax.dot_general(
        hi,
        jnp.concatenate([hi, lo], axis=1),
        (((0,), (0,)), ((), ())),
        preferred_element_type=f32,
    )


def whole_gram(halves):
    cross = halves[:, LANES:]
    return halves[:, :LANES] + (cross + cross.T)


def list_kernel(history_ref, positive_ref, out_ref, *, slots, rows_dev):
    shift = rows_dev.bit_length() - 1
    sq = (LANES, LANES)
    ids = jnp.concatenate(
        [history_ref[...], positive_ref[...], jnp.full((LANES - slots, LANES), -1, i32)], axis=0
    )
    owner_r = lax.shift_right_arithmetic(ids, shift)
    owner_c = owner_r.T
    local = ids & (rows_dev - 1)
    high_r = (lax.shift_right_logical(local, 6) + 1).astype(f32)
    low_r = (local & 63).astype(f32)
    users = iota2((1, LANES), 1).astype(f32)
    lane = iota2(sq, 1)
    sub = iota2(sq, 0)
    lane_f = lane.astype(f32)
    one = jnp.ones(sq, f32)
    zero = jnp.zeros(sq, f32)
    lower = jnp.concatenate([jnp.where(sub > lane, one, zero), one], axis=0).astype(bf16)
    ones = one.astype(bf16)
    carry = jnp.zeros(sq, f32)
    acc = jnp.zeros((3 * LANES, LANES), f32)
    for start in range(0, slots, GROUP):
        group = range(start, start + GROUP)
        members = [owner_c[:, h : h + 1] == lane for h in group]
        counts = dot_f32(
            lower,
            jnp.concatenate([jnp.where(m, one, zero) for m in members], axis=1).astype(bf16),
        )
        mine = []
        for k, member in enumerate(members):
            block = counts[:, k * LANES : (k + 1) * LANES]
            mine.append(jnp.where(member, block[:LANES] + carry, zero))
            carry = carry + block[LANES:]
        rank = dot_f32(jnp.concatenate(mine, axis=0).astype(bf16), ones)
        place = jnp.where(rank == jnp.concatenate([lane_f] * GROUP, axis=0), 1.0, 0.0)
        vals = []
        for h in group:
            at_owner = owner_r[h : h + 1, :] == sub
            code = users + (LANES if h == slots - 1 else 0)
            vals.append(
                jnp.concatenate(
                    [
                        jnp.where(at_owner, jnp.broadcast_to(value, sq), zero)
                        for value in (high_r[h : h + 1, :], low_r[h : h + 1, :], code)
                    ],
                    axis=0,
                )
            )
        acc = acc + dot_f32(jnp.concatenate(vals, axis=1).astype(bf16), place.astype(bf16))
    high = acc[:LANES].astype(i32)
    low = acc[LANES : 2 * LANES].astype(i32)
    code = acc[2 * LANES :].astype(i32)
    present = high > 0
    out_ref[:, 0, :] = jnp.where(present, (high - 1) * 64 + low, rows_dev).astype(f32)
    out_ref[:, 1, :] = jnp.where(present, code, -1).astype(f32)


def request_lists(history_ids, positive_ids, rows_dev):
    users, hist_len = history_ids.shape
    return pl.pallas_call(
        functools.partial(list_kernel, slots=hist_len + 1, rows_dev=rows_dev),
        out_shape=jax.ShapeDtypeStruct((LANES, 2, LANES), f32),
        name="request_lists",
    )(history_ids.T, positive_ids.reshape(1, users))


def partial_kernel(rows_ref, plane_ref, table_ref, codes_ref, gram_ref, *refs, first, first_step, takes):
    from_ref = refs[0] if takes else None
    out_refs = refs[int(takes) : -8]
    picked_refs = refs[-8:]
    code_of = iota2((2 * LANES, LANES), 0).astype(f32)
    one = jnp.ones((2 * LANES, LANES), f32)
    zero = jnp.zeros((2 * LANES, LANES), f32)
    unroll = 32
    offsets = (first + first_step * pl.program_id(0), 2 * pl.program_id(1))
    at_first = ((plane_ref[1] + offsets[0]) & 3) * plane_ref[4]
    for k in range(2):
        at_second = ((plane_ref[2] + (offsets[1] + k)) & 3) * plane_ref[5]
        for j in range(4):
            at_third = ((plane_ref[3] + j) & 3) * plane_ref[6]
            source = plane_ref[0] + at_first + at_second + at_third
            base = source * LANES
            picked_ref = picked_refs[4 * k + j]
            for at in range(0, LANES, unroll):
                picked = [
                    table_ref[pl.ds(rows_ref[base + (at + i)], 1), :] for i in range(unroll)
                ]
                for i in range(unroll):
                    picked_ref[at + i : at + i + 1, :] = picked[i]
            weight = jnp.where(codes_ref[pl.ds(source, 1), :] == code_of, one, zero)
            weight = weight.astype(bf16)
            block = dot_f32(
                jnp.concatenate([weight, weight], axis=1),
                jnp.concatenate(split2(picked_ref[...]), axis=0),
            )
            gram = jnp.broadcast_to(gram_ref[pl.ds(source, 1), :], (8, LANES))
            if from_ref is not None:
                block = block + from_ref[0, k, j, : 2 * LANES, :]
                gram = gram + from_ref[0, k, j, 2 * LANES :, :]
            if len(out_refs) == 2:
                out_refs[0][0, k, j] = block[:LANES]
                out_refs[1][0, k, j, :LANES, :] = block[LANES:]
                out_refs[1][0, k, j, LANES:, :] = gram
            else:
                out_refs[0][0, k, j, : 2 * LANES, :] = block
                out_refs[0][0, k, j, 2 * LANES :, :] = gram


def partial_sums(rows_idx, plane, table, codes, gram, firsts, received=None, place=0, split=False):
    rows_dev, width = table.shape
    n = len(firsts)
    block = (1, 2, 4, BLOCK_ROWS, width)
    sizes = (LANES, BLOCK_ROWS - LANES) if split else (BLOCK_ROWS,)

    def whole(shape):
        return pl.BlockSpec(shape, lambda i, k, r, p: (0,) * len(shape))

    in_specs = [whole((rows_dev, width)), whole(codes.shape), whole(gram.shape)]
    operands = (rows_idx, plane, table, codes, gram)
    if received is not None:
        in_specs.append(pl.BlockSpec(block, lambda i, k, r, p: (place, k, 0, 0, 0)))
        operands += (received,)
    return pl.pallas_call(
        functools.partial(
            partial_kernel,
            first=firsts[0],
            first_step=firsts[-1] - firsts[0],
            takes=received is not None,
        ),
        grid_spec=pltpu.PrefetchScalarGridSpec(
            num_scalar_prefetch=2,
            grid=(n, 2),
            in_specs=in_specs,
            out_specs=[
                pl.BlockSpec((1, 2, 4, size, width), lambda i, k, r, p: (i, k, 0, 0, 0))
                for size in sizes
            ],
            scratch_shapes=[pltpu.VMEM((LANES, width), f32)] * 8,
        ),
        out_shape=[jax.ShapeDtypeStruct((n, 4, 4, size, width), f32) for size in sizes],
        compiler_params=pltpu.CompilerParams(vmem_limit_bytes=32 * 2**20),
        name="partial_sums",
    )(*operands)


def split_sum_kernel(*refs):
    pieces, outs = refs[:-4], refs[-4:]
    for i in range(4):
        total = pieces[0][i]
        for piece in pieces[1:]:
            total = total + piece[i]
        outs[i][...] = total


def split_sums(pieces, name):
    return pl.pallas_call(
        split_sum_kernel,
        out_shape=[jax.ShapeDtypeStruct(pieces[0].shape[1:], f32)] * 4,
        compiler_params=pltpu.CompilerParams(vmem_limit_bytes=40 * 2**20),
        name=name,
    )(*pieces)


def add_rows_kernel(block_ref, part_ref, out_ref, *, start):
    end = start + part_ref.shape[2]
    for k in range(4):
        out_ref[k] = block_ref[k]
        out_ref[k, :, start:end, :] = block_ref[k, :, start:end, :] + part_ref[k]


def with_rows(block, part, start):
    return pl.pallas_call(
        functools.partial(add_rows_kernel, start=start),
        out_shape=jax.ShapeDtypeStruct(block.shape, f32),
        compiler_params=pltpu.CompilerParams(vmem_limit_bytes=24 * 2**20),
        name="add_relayed",
    )(block, part)


def along(stage, by):
    pairs = []
    for device in range(128):
        at = [device // 32, device // 16 % 2, device // 4 % 4, device % 4]
        axis = ORDERS[at[1]][stage]
        at[axis] = (at[axis] + by) % 4
        pairs.append((device, ((at[0] * 2 + at[1]) * 4 + at[2]) * 4 + at[3]))
    return pairs


def shifted(array, stage, by):
    return lax.ppermute(array, DP_ROWS, along(stage, by)) if by else array


def plane_of(core):
    here = jnp.stack([lax.axis_index(axis) for axis in DP_ROWS]).astype(i32)
    strides = jnp.array([32, 16, 4, 1], i32)
    orders = [jnp.array(order, i32) for order in ORDERS]
    order = jnp.where(core == 0, orders[0], orders[1])
    chosen = order[:, None] == jnp.arange(4, dtype=i32)[None, :]
    at = jnp.sum(jnp.where(chosen, here[None, :], 0), axis=1)
    stride = jnp.sum(jnp.where(chosen, strides[None, :], 0), axis=1)
    return jnp.concatenate([(core * 16)[None], at, stride])


def to_sources(rows_idx, table, codes, gram):
    core = lax.axis_index(CORE).astype(i32)
    other, own = plane_of(1 - core), plane_of(core)
    swap = [(0, 1), (1, 0)]
    received = []
    for firsts in ((1, 3), (2, 0)):
        (mine,) = partial_sums(rows_idx, other, table, codes, gram, firsts)
        received.append(lax.ppermute(mine, CORE, swap))

    def blocks(first, k, split=False):
        outs = partial_sums(
            rows_idx, own, table, codes, gram, (first,), received[k // 2], k % 2, split
        )
        return [out.reshape(out.shape[1:]) for out in outs]

    upper, lower = blocks(2, 2, True)
    upper, lower = shifted(upper, 0, 1), shifted(lower, 0, 3)
    (ahead,), (behind,), (here,) = blocks(1, 0), blocks(3, 1), blocks(0, 3)
    ahead = shifted(with_rows(ahead, upper, 0), 0, 1)
    behind = shifted(with_rows(behind, lower, LANES), 0, 3)
    pieces = [here, ahead, behind]
    for stage in (1, 2):
        parts = split_sums(pieces, f"sum_stage_{stage}")
        pieces = [shifted(part, stage, by) for by, part in enumerate(parts)]
    return pieces


def user_kernel(*refs, hist_len):
    out_ref = refs[4]
    sums = (refs[0][...] + refs[1][...]) + (refs[2][...] + refs[3][...])
    user = sums[:LANES] / hist_len
    positive = sums[LANES : 2 * LANES]
    gap = jnp.sum(user * positive, axis=1, keepdims=True) - 1.0
    sq = (LANES, LANES)
    gap_row = jnp.sum(
        jnp.where(iota2(sq, 0) == iota2(sq, 1), jnp.broadcast_to(gap, sq), 0.0),
        axis=0,
        keepdims=True,
    )
    out_ref[:LANES, :] = positive
    out_ref[LANES : 2 * LANES, :] = user
    tail = (8, LANES)
    out_ref[2 * LANES :, :] = jnp.where(
        iota2(tail, 0) == 0,
        jnp.broadcast_to(gap_row, tail),
        sums[2 * LANES :],
    )


def user_block(pieces, hist_len):
    return pl.pallas_call(
        functools.partial(user_kernel, hist_len=hist_len),
        out_shape=jax.ShapeDtypeStruct(pieces[0].shape, f32),
        name="user_block",
    )(*pieces)


def update_kernel(
    row_idx_ref, src_idx_ref, blocks_ref, item_ref, table_ref, state_hbm, new_table_ref, new_state_ref,
    stage_ref, gram_ref, total_ref, state_ref, state_sem, *acc_refs, sources, coef, hist_len,
):
    fetch_state = pltpu.make_async_copy(state_hbm, state_ref, state_sem)
    g = pl.program_id(0)
    rows_dev = table_ref.shape[0]
    sq = (LANES, LANES)

    @pl.when(g == 0)
    def _():
        fetch_state.start()
        gram_ref[...] = jnp.zeros_like(gram_ref)
        for acc in acc_refs:
            acc[...] = jnp.zeros_like(acc)
        total_ref[...] = item_ref[:, 0, 1, :]

    diagonal = iota2(sq, 0) == iota2(sq, 1)
    users = jnp.concatenate(
        [blocks_ref[s, LANES : 2 * LANES, :] for s in range(sources)], axis=0
    )
    pulls = dot_split(users, total_ref[...])
    for s in range(sources):
        user = blocks_ref[s, LANES : 2 * LANES, :]
        gap_row = blocks_ref[s, 2 * LANES : 2 * LANES + 1, :]
        gap = 2.0 * jnp.sum(
            jnp.where(diagonal, jnp.broadcast_to(gap_row, sq), 0.0), axis=1, keepdims=True
        )
        pull = pulls[LANES * s : LANES * (s + 1)]
        grad = gap * blocks_ref[s, :LANES, :] + 2.0 * coef * pull
        stage_ref[2 * LANES * s : 2 * LANES * s + LANES, :] = grad / hist_len
        stage_ref[2 * LANES * s + LANES : 2 * LANES * (s + 1), :] = gap * user
    gram_ref[...] += half_gram(users)

    base = g * (sources * LANES)
    unroll = 128

    def body(j, carry):
        for at in range(0, unroll, CHAINS):
            first = base + j * unroll + at
            rows = [row_idx_ref[first + k] for k in range(CHAINS)]
            srcs = [src_idx_ref[first + k] for k in range(CHAINS)]
            grads = [stage_ref[pl.ds(srcs[k], 1), :] for k in range(CHAINS)]
            sums = [acc_refs[k][pl.ds(rows[k], 1), :] + grads[k] for k in range(CHAINS)]
            for k in range(CHAINS):
                acc_refs[k][pl.ds(rows[k], 1), :] = sums[k]
        return carry

    lax.fori_loop(0, sources * LANES // unroll, body, 0)

    @pl.when(g == pl.num_programs(0) - 1)
    def _():
        fetch_state.wait()
        step = 512
        gram = whole_gram(gram_ref[...])

        def finish(i, carry):
            at = pl.ds(pl.multiple_of(i * step, step), step)
            table = table_ref[at, :]
            grad = 2.0 * coef * dot_split(table, gram)
            for acc in acc_refs:
                grad = grad + acc[at, :]
            new_state = state_ref[at, :] + grad * grad
            new_state_ref[at, :] = new_state
            new_table_ref[at, :] = table - step_size * grad / jnp.sqrt(new_state)
            return carry

        lax.fori_loop(0, rows_dev // step, finish, 0)


def update_rows(row_idx, src_idx, blocks, table, state, coef, hist_len):
    rows_dev, width = table.shape
    devices = blocks.shape[0]
    sources = 16
    whole = pl.BlockSpec((rows_dev, width), lambda g, r, s: (0, 0))
    return pl.pallas_call(
        functools.partial(update_kernel, sources=sources, coef=coef, hist_len=hist_len),
        grid_spec=pltpu.PrefetchScalarGridSpec(
            num_scalar_prefetch=2,
            grid=(devices // sources,),
            in_specs=[
                pl.BlockSpec((sources, BLOCK_ROWS, width), lambda g, r, s: (g, 0, 0)),
                pl.BlockSpec((devices, 1, 8, width), lambda g, r, s: (0, 2 * LANES // 8, 0, 0)),
                whole,
                pl.BlockSpec(memory_space=pltpu.HBM),
            ],
            out_specs=[whole, whole],
            scratch_shapes=[
                pltpu.VMEM((sources * 2 * LANES, width), f32),
                pltpu.VMEM((width, 2 * width), f32),
                pltpu.VMEM((width, width), f32),
                pltpu.VMEM((rows_dev, width), f32),
                pltpu.SemaphoreType.DMA,
            ]
            + [pltpu.VMEM((rows_dev + 8, width), f32)] * CHAINS,
        ),
        out_shape=(
            jax.ShapeDtypeStruct((rows_dev, width), f32),
            jax.ShapeDtypeStruct((rows_dev, width), f32),
        ),
        compiler_params=pltpu.CompilerParams(vmem_limit_bytes=48 * 2**20),
        name="update_rows",
    )(row_idx, src_idx, blocks, blocks.reshape(devices, BLOCK_ROWS // 8, 8, width), table, pltpu.with_memory_space_constraint(state, pltpu.HBM))


def shards(item_table, adagrad_state, history_ids, positive_ids):
    rows_dev, width = item_table.shape
    users_dev, hist_len = history_ids.shape
    devices = lax.axis_size(DP_ROWS)
    coef = penalty_weight / (rows_dev * devices)
    item_gram = jnp.dot(
        item_table.T,
        item_table,
        precision=lax.Precision.HIGHEST,
        preferred_element_type=f32,
    )
    lists = request_lists(history_ids, positive_ids, rows_dev)
    asked = lax.all_to_all(lists, DP_ROWS, split_axis=0, concat_axis=0, tiled=True)
    rows = asked[:, 0, :].astype(i32).reshape(-1)
    codes = asked[:, 1, :]
    place = jnp.arange(devices * LANES, dtype=i32) // LANES % 16 * (2 * LANES)
    src_idx = place + jnp.maximum(codes.astype(i32).reshape(-1), 0)
    pieces = to_sources(jnp.where(rows < rows_dev, rows, 0), item_table, codes, item_gram)
    block = user_block(pieces, hist_len)
    blocks = lax.all_gather(block, DP_ROWS)
    return update_rows(rows, src_idx, blocks, item_table, adagrad_state, coef, hist_len)


def solution(mesh):
    finer = Mesh(mesh.devices.reshape(4, 2, 4, 4), DP_ROWS)
    rows = P(DP_ROWS, None)
    return jax.shard_map(
        shards,
        mesh=finer,
        in_specs=(rows, rows, rows, P(DP_ROWS)),
        out_specs=(rows, rows),
        check_vma=False,
    )
```
